512 devices in a mesh: lon: 32 (over z_lo, y), lat: 16 (over x, z_hi, core).
Axes of the slice: x: 4, y: 4, z: 16 (z_hi: 2, z_lo: 8; z = z_hi * 8 + z_lo), core: 2. Of those that a mesh axis runs over, the one named last changes fastest.
Arguments:
- queries: bfloat16 [16, 32, 384, 128], P('lat', 'lon'), may hold values from -4.6 to 4.6
- keys: bfloat16 [16, 32, 384, 128], P('lat', 'lon'), may hold values from -4.6 to 4.6
- values: bfloat16 [16, 32, 384, 128], P('lat', 'lon'), may hold values from -6 to 6
- cotangent: bfloat16 [16, 32, 384, 128], P('lat', 'lon'), may hold values from -384 to 384
- key_tiles: int32 [16, 32, 21], replicated, may hold values from 0 to 511, as said below
- tile_count: int32 [16, 32], replicated, may hold values from 2 to 21, as said below
Outputs:
- grad_queries: bfloat16 [16, 32, 384, 128], P('lat', 'lon')
- grad_keys: bfloat16 [16, 32, 384, 128], P('lat', 'lon')
- grad_values: bfloat16 [16, 32, 384, 128], P('lat', 'lon')
The draws below stay inside these ranges and needn't reach their ends.
Inputs may be any that keep to these rules, and one draw needn't show every extreme that they name: `key_tiles`: entries are tile ids. The first tile_count entries of tile (a, b) are distinct, include (a, b) itself, and name tiles of bands a - 1 to a + 1 whose longitude lies within 3 tiles of b around the cycle; later entries are tile ids. `tile_count`: some tiles list all 21 entries.
All inputs are finite; a program needn't handle non-finite values.
Results may differ from the reference program's by a relative error of at most 0.0067.
Values may be sent and summed in bfloat16 or wider, within the bound.
No kernel may reach another device: no remote copies, remote signals or barrier semaphores. Data moves between devices by JAX's collectives and lax.ppermute only.
A program may use at most 64 MiB of HBM per device.

```python
import jax
import jax.numpy as jnp
from jax import lax

HD = 128
TOK_DEV = 384
REACH = 3
SLOTS = 21
LAT_TILES = 16
LON_TILES = 32


def drawn_entries(key):
    array_shape = (LAT_TILES, LON_TILES, TOK_DEV, HD)
    return jnp.clip(jax.random.normal(key, array_shape, jnp.float32), -4.6, 4.6)


def draw_queries(key, part):
    entries = drawn_entries(jax.random.fold_in(key, 3))
    return entries.astype(jnp.bfloat16)


def draw_keys(key, part):
    entries = drawn_entries(jax.random.fold_in(key, 4))
    return entries.astype(jnp.bfloat16)


def tile_plan(key):
    base_key = jax.random.fold_in(key, 97)
    window_len = 2 * REACH + 1
    slot_count = 3 * window_len
    full_shape = (LAT_TILES, LON_TILES, slot_count)
    band_index = jnp.arange(LAT_TILES)[:, None, None]
    column_index = jnp.arange(LON_TILES)[None, :, None]
    candidate = jnp.arange(slot_count)[None, None, :]
    cand_band = band_index + candidate // window_len - 1
    cand_column = (column_index + candidate % window_len - REACH) % LON_TILES
    inside = jnp.broadcast_to((cand_band >= 0) & (cand_band < LAT_TILES), full_shape)
    cand_ids = jnp.broadcast_to(jnp.clip(cand_band, 0, LAT_TILES - 1) * LON_TILES + cand_column, full_shape)
    self_id = jnp.broadcast_to(band_index * LON_TILES + column_index, full_shape)
    priority = jax.random.randint(jax.random.fold_in(base_key, 1), full_shape, 0, 4096)
    rank_score = priority * slot_count + candidate
    rank_score = jnp.where(candidate == window_len + REACH, -1, rank_score)
    rank_score = jnp.where(inside, rank_score, 4096 * slot_count + candidate)
    ranking = jnp.argsort(rank_score, axis=-1)
    listed_ids = jnp.take_along_axis(jnp.where(inside, cand_ids, self_id), ranking, axis=-1)
    valid_count = jnp.sum(inside.astype(jnp.int32), axis=-1)
    band_row = jnp.arange(LAT_TILES)
    pole_gap = jnp.minimum(band_row, LAT_TILES - 1 - band_row)[:, None]
    ceiling = jnp.maximum(3, slot_count - 3 * (pole_gap - 1))
    least = jnp.maximum(2, ceiling // 2)
    raw_pick = jax.random.randint(jax.random.fold_in(base_key, 2), (LAT_TILES, LON_TILES), 0, 1 << 20)
    middle_count = least + raw_pick % (ceiling - least + 1)
    trim_pick = jax.random.randint(jax.random.fold_in(base_key, 3), (LAT_TILES, LON_TILES), 0, 3)
    first_column = jnp.arange(LON_TILES)[None, :] == 0
    polar_count = valid_count - jnp.where(first_column, 0, trim_pick)
    counted = jnp.where(pole_gap <= 1, polar_count, jnp.minimum(middle_count, valid_count))
    return (listed_ids.astype(jnp.int32), counted.astype(jnp.int32))


def draw_key_tiles(key, part):
    return tile_plan(key)[0]


def draw_tile_count(key, part):
    return tile_plan(key)[1]


def block_levels(rng, extent, pieces, low, largest):
    level = 1.0
    for dim, parts in pieces:
        steps = jax.random.uniform(jax.random.fold_in(jax.random.fold_in(rng, 6), dim), (parts,), jnp.float32, low / len(pieces), largest / len(pieces))
        level = level * jnp.repeat(jnp.exp(steps), extent[dim] // parts).reshape((-1,) + (1,) * (len(extent) - 1 - dim))
    return level


def centred(key, shape, width, bound, cuts=(), kind=jnp.bfloat16):
    result = jax.random.normal(key, shape, jnp.float32) * width
    if len(cuts) > 0:
        result = block_levels(key, shape, cuts, -0.22, 0.18) * result
    return jnp.clip(result, min=-bound, max=bound).astype(kind)


def setup_inputs(seed: int = 0) -> dict:
    streams_of = jax.random.split(jax.random.key(seed), 7)
    return {
        "queries": draw_queries(jax.random.fold_in(streams_of[6], 71), 0),
        "keys": draw_keys(jax.random.fold_in(streams_of[6], 71), 0),
        "values": centred(streams_of[2], (LAT_TILES, LON_TILES, TOK_DEV, HD), 1.0, 6.0, ((0, 16), (1, 32))),
        "cotangent": centred(streams_of[3], (LAT_TILES, LON_TILES, TOK_DEV, HD), 64.0, 384.0, ((0, 16), (1, 32))),
        "key_tiles": draw_key_tiles(jax.random.fold_in(streams_of[6], 71), 0),
        "tile_count": draw_tile_count(jax.random.fold_in(streams_of[6], 71), 0),
    }


NEG_BIG = -1.0e30


def reference(queries, keys, values, cotangent, key_tiles, tile_count):
    tiles = LAT_TILES * LON_TILES
    score_scale = HD ** -0.5
    flat_q = queries.reshape(tiles, TOK_DEV, HD)
    flat_k = keys.reshape(tiles, TOK_DEV, HD)
    flat_v = values.reshape(tiles, TOK_DEV, HD)
    flat_g = cotangent.reshape(tiles, TOK_DEV, HD)
    tile_table = key_tiles.reshape(tiles, SLOTS)
    tile_totals = tile_count.reshape(tiles)

    def per_tile(state_now, position):
        grad_k, grad_v = state_now
        chosen = tile_table[position]
        slot_live = jnp.arange(SLOTS, dtype=jnp.int32) < tile_totals[position]
        tile_queries = flat_q[position].astype(jnp.float32)
        tile_grads = flat_g[position].astype(jnp.float32)
        key_set = flat_k[chosen].astype(jnp.float32)
        value_set = flat_v[chosen].astype(jnp.float32)
        logits = jnp.einsum("qd,skd->qsk", tile_queries, key_set) * score_scale
        logits = jnp.where(slot_live[None, :, None], logits, NEG_BIG)
        row_max = jnp.max(logits, axis=(1, 2))
        row_sum = jnp.sum(jnp.exp(logits - row_max[:, None, None]), axis=(1, 2))
        log_norm = row_max + jnp.log(row_sum)
        probs = jnp.exp(logits - log_norm[:, None, None])
        grad_prob = jnp.einsum("qd,skd->qsk", tile_grads, value_set)
        delta_rows = jnp.sum(probs * grad_prob, axis=(1, 2))
        grad_logit = lax.optimization_barrier((probs * (grad_prob - delta_rows[:, None, None])).astype(jnp.bfloat16)).astype(jnp.float32)
        probs_low = lax.optimization_barrier(probs.astype(jnp.bfloat16)).astype(jnp.float32)
        grad_query = jnp.einsum("qsk,skd->qd", grad_logit, key_set) * score_scale
        key_part = jnp.einsum("qsk,qd->skd", grad_logit, tile_queries) * score_scale
        value_part = jnp.einsum("qsk,qd->skd", probs_low, tile_grads)
        key_part = jnp.where(slot_live[:, None, None], key_part, 0.0)
        value_part = jnp.where(slot_live[:, None, None], value_part, 0.0)
        grad_k = grad_k.at[chosen].add(key_part)
        grad_v = grad_v.at[chosen].add(value_part)
        return (grad_k, grad_v), grad_query

    start = jnp.zeros((tiles, TOK_DEV, HD), jnp.float32)
    (grad_k, grad_v), grad_q = lax.scan(per_tile, (start, start), jnp.arange(tiles, dtype=jnp.int32))
    shape_out = (LAT_TILES, LON_TILES, TOK_DEV, HD)
    return (grad_q.reshape(shape_out).astype(jnp.bfloat16), grad_k.reshape(shape_out).astype(jnp.bfloat16), grad_v.reshape(shape_out).astype(jnp.bfloat16))
```

```python
import jax
import jax.numpy as jnp
from jax import lax
from jax.experimental import pallas as pl
from jax.experimental.pallas import tpu as pltpu
from jax.sharding import PartitionSpec as P

Y = 4
ZL = 8
LON = 32
LAT = 16
TOK = 384
HD = 128
SLOTS = 8
NEG_BIG = -1e30
AXES = ("lon", "lat")
CHUNK = 128


def cross_of(lat):
    other = lat + 1 if lat % 2 else lat - 1
    return other if 0 <= other < LAT else None


def pairs_of(rule):
    pairs = []
    for lon in range(LON):
        for lat in range(LAT):
            to = rule(lon // Y, lon % Y, lat)
            if to is not None:
                z, y, band = to
                pairs.append((lon * LAT + lat, (z * Y + y) * LAT + band))
    return pairs


def swap_rule(z, y, lat):
    return (z, y, lat ^ 1)


def cross_rule(z, y, lat):
    other = cross_of(lat)
    return None if other is None else (z, y, other)


def z_rule(step):
    unused = 0 if step > 0 else Y - 1

    def rule(z, y, lat):
        return None if y == unused else ((z + step) % ZL, y, lat)

    return rule


def far_z_rule(step):
    unused = 0 if step > 0 else Y - 1

    def rule(z, y, lat):
        if y == unused:
            return None
        if 0 <= z + step < ZL:
            return (z + step, y, lat)
        other = cross_of(lat)
        return None if other is None else ((z + step) % ZL, y, other)

    return rule


def permuted(x, rule):
    return lax.ppermute(x, AXES, pairs_of(rule))


def spread_y(here, before, after, my_y):
    pieces = [
        jnp.stack([here, jnp.where(peer < my_y, before, after)]) for peer in range(Y)
    ]
    groups = [[z * Y + y for y in range(Y)] for z in range(ZL)]
    return lax.all_to_all(
        jnp.stack(pieces), "lon", 0, 0, axis_index_groups=groups, tiled=True
    )


def spread_own(here, my_y):
    before = permuted(here, z_rule(1))
    after = permuted(here, z_rule(-1))
    return spread_y(here, before, after, my_y)


def spread_far(here, far, my_z, my_y):
    before = permuted(jnp.where(my_z == ZL - 1, here, far), far_z_rule(1))
    after = permuted(jnp.where(my_z == 0, here, far), far_z_rule(-1))
    return spread_y(far, before, after, my_y)


def slot_columns(my_z, my_y):
    sender = jnp.arange(Y, dtype=jnp.int32)
    near = my_z * Y + sender
    beside = (my_z + jnp.where(sender > my_y, -1, 1)) % ZL * Y + sender
    columns = jnp.stack([near, beside], axis=1).reshape(SLOTS)
    real = jnp.stack([sender >= 0, sender != my_y], axis=1).reshape(SLOTS)
    return columns, real


NT = (((1,), (1,)), ((), ()))
NN = (((1,), (0,)), ((), ()))
TN = (((0,), (0,)), ((), ()))


def dot(a, b, dims):
    return lax.dot_general(a, b, dims, preferred_element_type=jnp.float32)


def stats_kernel(scale, last, live, q_ref, g_ref, kv_ref, st_in, st_out, *finals):
    st_out[...] = st_in[...]

    def visit(slot, carry):
        @pl.when(live[slot] != 0)
        def _():
            for part in range(TOK // CHUNK):
                rows = pl.ds(part * CHUNK, CHUNK)
                logit = dot(kv_ref[slot, 0, rows, :], q_ref[...], NT) * scale
                grad_prob = dot(kv_ref[slot, 1, rows, :], g_ref[...], NT)
                logit = logit.reshape(CHUNK // 8, 8, TOK)
                grad_prob = grad_prob.reshape(CHUNK // 8, 8, TOK)
                old_max = st_out[0]
                new_max = jnp.maximum(old_max, jnp.max(logit, axis=0))
                rescale = jnp.exp(old_max - new_max)
                power = jnp.exp(logit - new_max[None])
                st_out[0] = new_max
                st_out[1] = st_out[1] * rescale + jnp.sum(power, axis=0)
                st_out[2] = st_out[2] * rescale + jnp.sum(power * grad_prob, axis=0)

        return carry

    lax.fori_loop(0, SLOTS, visit, 0)
    if last:
        top = jnp.max(st_out[0], axis=0, keepdims=True)
        weight = jnp.exp(st_out[0] - top)
        total = jnp.sum(st_out[1] * weight, axis=0, keepdims=True)
        weighted = jnp.sum(st_out[2] * weight, axis=0, keepdims=True)
        finals[0][0:1, :] = top + jnp.log(total)
        finals[0][1:2, :] = weighted / total


def query_kernel(scale, live, stat_ref, q_ref, g_ref, own_ref, mate_ref, far_ref, out_ref, acc, low):
    acc[...] = jnp.zeros_like(acc)
    norm = stat_ref[0:1, :]
    delta = stat_ref[1:2, :]
    for group, kv_ref in enumerate((own_ref, mate_ref, far_ref)):

        def visit(slot, carry, group=group, kv_ref=kv_ref):
            @pl.when(live[group * SLOTS + slot] != 0)
            def _():
                for part in range(TOK // CHUNK):
                    rows = pl.ds(part * CHUNK, CHUNK)
                    logit = dot(kv_ref[slot, 0, rows, :], q_ref[...], NT) * scale
                    prob = jnp.exp(logit - norm)
                    grad_prob = dot(kv_ref[slot, 1, rows, :], g_ref[...], NT)
                    low[rows, :] = (prob * (grad_prob - delta)).astype(jnp.bfloat16)
                acc[...] += dot(kv_ref[slot, 0], low[...], TN)

            return carry

        lax.fori_loop(0, SLOTS, visit, 0)
    out_ref[...] = (acc[...].T * scale).astype(jnp.bfloat16)


def key_kernel(scale, last, off, live, k_ref, v_ref, qg_ref, stat_ref, acc_in, *rest):
    outs, (prob_low, grad_low) = rest[:-2], rest[-2:]
    if last:
        dk_out, dv_out, acc = outs[0], outs[1], outs[2]
    else:
        acc = outs[0]
    acc[...] = acc_in[...]

    def visit(slot, carry):
        @pl.when(live[slot] != 0)
        def _():
            norm = stat_ref[slot, 0:1, :]
            delta = stat_ref[slot, 1:2, :]
            for part in range(TOK // CHUNK):
                rows = pl.ds(part * CHUNK, CHUNK)
                logit = dot(k_ref[rows, :], qg_ref[slot, off], NT) * scale
                prob = jnp.exp(logit - norm)
                grad_prob = dot(v_ref[rows, :], qg_ref[slot, off + 1], NT)
                prob_low[rows, :] = prob.astype(jnp.bfloat16)
                grad_low[rows, :] = (prob * (grad_prob - delta)).astype(jnp.bfloat16)
            acc[0] += dot(grad_low[...], qg_ref[slot, off], NN)
            acc[1] += dot(prob_low[...], qg_ref[slot, off + 1], NN)

        return carry

    lax.fori_loop(0, SLOTS, visit, 0)
    if last:
        dk_out[...] = (acc[0] * scale).astype(jnp.bfloat16)
        dv_out[...] = acc[1].astype(jnp.bfloat16)


SMEM = pl.BlockSpec(memory_space=pltpu.SMEM)
VMEM = pl.BlockSpec(memory_space=pltpu.VMEM)


def params():
    return pltpu.CompilerParams(vmem_limit_bytes=40 * 1024 * 1024)


def cost(pairs, matmuls):
    return pl.CostEstimate(
        flops=pairs * matmuls * 2 * TOK * TOK * HD,
        transcendentals=pairs * TOK * TOK,
        bytes_accessed=pairs * 4 * TOK * HD * 2,
    )


def run_stats(scale, live, q, g, kv, state, last):
    state_shape = jax.ShapeDtypeStruct((3, 8, TOK), jnp.float32)
    stat_shape = jax.ShapeDtypeStruct((2, TOK), jnp.float32)

    def body(*refs):
        stats_kernel(scale, last, *refs)

    return pl.pallas_call(
        body,
        out_shape=(state_shape, stat_shape) if last else (state_shape,),
        in_specs=[SMEM, VMEM, VMEM, VMEM, VMEM],
        out_specs=(VMEM, VMEM) if last else (VMEM,),
        compiler_params=params(),
        cost_estimate=cost(SLOTS, 2),
        name="row_stats",
    )(live, q, g, kv, state)


def run_query(scale, live, stat, q, g, groups):
    def body(*refs):
        query_kernel(scale, *refs)

    return pl.pallas_call(
        body,
        out_shape=jax.ShapeDtypeStruct((TOK, HD), jnp.bfloat16),
        in_specs=[SMEM] + [VMEM] * 6,
        out_specs=VMEM,
        scratch_shapes=[
            pltpu.VMEM((HD, TOK), jnp.float32),
            pltpu.VMEM((TOK, TOK), jnp.bfloat16),
        ],
        compiler_params=params(),
        cost_estimate=cost(3 * SLOTS, 3),
        name="grad_query",
    )(live, stat, q, g, *groups)


def run_key(scale, live, k, v, qg, off, stats, acc, last):
    acc_shape = jax.ShapeDtypeStruct((2, TOK, HD), jnp.float32)
    low_shape = jax.ShapeDtypeStruct((TOK, HD), jnp.bfloat16)

    def body(*refs):
        key_kernel(scale, last, off, *refs)

    return pl.pallas_call(
        body,
        out_shape=(low_shape, low_shape, acc_shape) if last else (acc_shape,),
        in_specs=[SMEM] + [VMEM] * 5,
        out_specs=(VMEM, VMEM, VMEM) if last else (VMEM,),
        scratch_shapes=[
            pltpu.VMEM((TOK, TOK), jnp.bfloat16),
            pltpu.VMEM((TOK, TOK), jnp.bfloat16),
        ],
        compiler_params=params(),
        cost_estimate=cost(SLOTS, 4),
        name="grad_key",
    )(live, k, v, qg, stats, acc)


def per_device(queries, keys, values, cotangent, key_tiles, tile_count):
    scale = HD ** (-0.5)
    my_lat = lax.axis_index("lat")
    my_lon = lax.axis_index("lon")
    my_z, my_y = my_lon // Y, my_lon % Y
    q = queries.reshape(TOK, HD)
    k = keys.reshape(TOK, HD)
    v = values.reshape(TOK, HD)
    g = cotangent.reshape(TOK, HD)

    columns, real = slot_columns(my_z, my_y)
    far_lat = jnp.where(my_lat % 2 == 1, my_lat + 1, my_lat - 1)
    bands = jnp.stack([my_lat, my_lat ^ 1, far_lat])
    band_real = (bands >= 0) & (bands < LAT)
    ids = (bands[:, None] * LON + columns[None, :]).reshape(-1)
    slot_real = (band_real[:, None] & real[None, :]).reshape(-1)
    table = key_tiles.reshape(LAT * LON, -1)
    totals = tile_count.reshape(-1)
    places = jnp.arange(table.shape[1], dtype=jnp.int32)
    own_id = my_lat * LON + my_lon
    own_list = lax.dynamic_index_in_dim(table, own_id, 0, keepdims=False)
    own_total = lax.dynamic_index_in_dim(totals, own_id, 0, keepdims=False)
    i_list = jnp.any(
        (own_list[None, :] == ids[:, None]) & (places < own_total)[None, :], axis=1
    )
    safe = jnp.clip(ids, 0, LAT * LON - 1)
    lists_me = jnp.any(
        (table[safe] == own_id) & (places[None, :] < totals[safe][:, None]), axis=1
    )
    live_keys = (i_list & slot_real).astype(jnp.int32)
    live_queries = (lists_me & slot_real).astype(jnp.int32)

    kv = jnp.stack([k, v])
    qg = jnp.stack([q, g])
    kvqg = jnp.concatenate([kv, qg])
    far_kv = permuted(kv, cross_rule)
    own = spread_own(kvqg, my_y).reshape(SLOTS, 4, TOK, HD)
    far_kvs = spread_far(kv, far_kv, my_z, my_y).reshape(SLOTS, 2, TOK, HD)
    mate = permuted(own, swap_rule)
    far_qg = permuted(qg, cross_rule)
    far_qgs = spread_far(qg, far_qg, my_z, my_y).reshape(SLOTS, 2, TOK, HD)

    live_k = live_keys.reshape(3, SLOTS)
    live_q = live_queries.reshape(3, SLOTS)
    blank = jnp.zeros((8, TOK), jnp.float32)
    state = jnp.stack([blank + NEG_BIG, blank, blank])
    (state,) = run_stats(scale, live_k[0], q, g, own, state, False)
    (state,) = run_stats(scale, live_k[1], q, g, mate, state, False)
    _, stat = run_stats(scale, live_k[2], q, g, far_kvs, state, True)

    own_stats = spread_own(stat, my_y).reshape(SLOTS, 2, TOK)
    far_stats = permuted(own_stats, cross_rule)
    mate_stats = permuted(own_stats, swap_rule)
    grad_query = run_query(scale, live_keys, stat, q, g, (own, mate, far_kvs))

    acc = jnp.zeros((2, TOK, HD), jnp.float32)
    (acc,) = run_key(scale, live_q[0], k, v, own, 2, own_stats, acc, False)
    (acc,) = run_key(scale, live_q[1], k, v, mate, 2, mate_stats, acc, False)
    grad_key, grad_value, _ = run_key(
        scale, live_q[2], k, v, far_qgs, 0, far_stats, acc, True
    )
    out_shape = (1, 1, TOK, HD)
    return (
        grad_query.reshape(out_shape),
        grad_key.reshape(out_shape),
        grad_value.reshape(out_shape),
    )


def solution(mesh):
    tile = P("lat", "lon", None, None)
    return jax.shard_map(
        per_device,
        mesh=mesh,
        in_specs=(tile, tile, tile, tile, P(), P()),
        out_specs=(tile, tile, tile),
        check_vma=False,
    )
```

```python
import jax
import jax.numpy as jnp
from jax import lax
from jax.experimental import pallas as pl
from jax.experimental.pallas import tpu as pltpu
from jax.sharding import PartitionSpec as P


Y = 4
ZL = 8
LON = 32
LAT = 16
TOK = 384
HD = 128
SLOTS = 8
NEG_BIG = -1e30
AXES = ("lon", "lat")
CHUNK = 128
STAT_ROWS = 32
PACK = 2 * TOK + STAT_ROWS


def cross_of(lat):
    other = lat + 1 if lat % 2 else lat - 1
    return other if 0 <= other < LAT else None


def pairs_of(rule):
    pairs = []
    for lon in range(LON):
        for lat in range(LAT):
            to = rule(lon // Y, lon % Y, lat)
            if to is not None:
                z, y, band = to
                pairs.append((lon * LAT + lat, (z * Y + y) * LAT + band))
    return pairs


def swap_rule(z, y, lat):
    return (z, y, lat ^ 1)


def cross_rule(z, y, lat):
    other = cross_of(lat)
    return None if other is None else (z, y, other)


def z_rule(step):
    unused = 0 if step > 0 else Y - 1

    def rule(z, y, lat):
        return None if y == unused else ((z + step) % ZL, y, lat)

    return rule


def far_z_rule(step):
    unused = 0 if step > 0 else Y - 1

    def rule(z, y, lat):
        if y == unused:
            return None
        if 0 <= z + step < ZL:
            return (z + step, y, lat)
        other = cross_of(lat)
        return None if other is None else ((z + step) % ZL, y, other)

    return rule


def permuted(x, rule):
    return lax.ppermute(x, AXES, pairs_of(rule))


def pack_kernel(my_y, here, before, after, out, sems):
    def near(peer):
        return pltpu.make_async_copy(here, out.at[peer, 0], sems.at[2 * peer])

    def beside(peer, source):
        return pltpu.make_async_copy(source, out.at[peer, 1], sems.at[2 * peer + 1])

    for peer in range(Y):
        near(peer).start()

        @pl.when(peer < my_y[0])
        def _():
            beside(peer, before).start()

        @pl.when(peer >= my_y[0])
        def _():
            beside(peer, after).start()

    for peer in range(Y):
        near(peer).wait()
        beside(peer, after).wait()


def run_pack(my_y, here, before, after):
    anywhere = pl.BlockSpec(memory_space=pl.ANY)
    return pl.pallas_call(
        pack_kernel,
        out_shape=jax.ShapeDtypeStruct((Y, 2) + here.shape, here.dtype),
        in_specs=[pl.BlockSpec(memory_space=pltpu.SMEM)] + [anywhere] * 3,
        out_specs=anywhere,
        scratch_shapes=[pltpu.SemaphoreType.DMA((2 * Y,))],
        name="pack",
    )(my_y.reshape(1), here, before, after)


def spread_y(here, before, after, my_y):
    groups = [[z * Y + y for y in range(Y)] for z in range(ZL)]
    payload = run_pack(my_y, here, before, after)
    got = lax.all_to_all(
        payload, "lon", 0, 0, axis_index_groups=groups, tiled=True
    )
    return got.reshape((SLOTS,) + here.shape)


def spread_own(here, my_y):
    before = permuted(here, z_rule(1))
    after = permuted(here, z_rule(-1))
    return spread_y(here, before, after, my_y)


def spread_far(here, far, my_z, my_y):
    before = permuted(jnp.where(my_z == ZL - 1, here, far), far_z_rule(1))
    after = permuted(jnp.where(my_z == 0, here, far), far_z_rule(-1))
    return spread_y(far, before, after, my_y)


def slot_columns(my_z, my_y):
    sender = jnp.arange(Y, dtype=jnp.int32)
    near = my_z * Y + sender
    beside = (my_z + jnp.where(sender > my_y, -1, 1)) % ZL * Y + sender
    columns = jnp.stack([near, beside], axis=1).reshape(SLOTS)
    real = jnp.stack([sender >= 0, sender != my_y], axis=1).reshape(SLOTS)
    return columns, real


NT = (((1,), (1,)), ((), ()))
NN = (((1,), (0,)), ((), ()))
TN = (((0,), (0,)), ((), ()))


def dot(a, b, dims):
    return lax.dot_general(a, b, dims, preferred_element_type=jnp.float32)


def stats_kernel(scale, last, live, q_ref, g_ref, kv_ref, st_in, st_out, *finals):
    st_out[...] = st_in[...]

    def visit(slot, carry):
        @pl.when(live[slot] != 0)
        def _():
            for part in range(TOK // CHUNK):
                rows = pl.ds(part * CHUNK, CHUNK)
                logit = dot(kv_ref[slot, 0, rows, :], q_ref[...], NT) * scale
                grad_prob = dot(kv_ref[slot, 1, rows, :], g_ref[...], NT)
                logit = logit.reshape(CHUNK // 8, 8, TOK)
                grad_prob = grad_prob.reshape(CHUNK // 8, 8, TOK)
                old_max = st_out[0]
                new_max = jnp.maximum(old_max, jnp.max(logit, axis=0))
                rescale = jnp.exp(old_max - new_max)
                power = jnp.exp(logit - new_max[None])
                st_out[0] = new_max
                st_out[1] = st_out[1] * rescale + jnp.sum(power, axis=0)
                st_out[2] = st_out[2] * rescale + jnp.sum(power * grad_prob, axis=0)

        return carry

    lax.fori_loop(0, SLOTS, visit, 0)
    if last:
        top = jnp.max(st_out[0], axis=0, keepdims=True)
        weight = jnp.exp(st_out[0] - top)
        total = jnp.sum(st_out[1] * weight, axis=0, keepdims=True)
        weighted = jnp.sum(st_out[2] * weight, axis=0, keepdims=True)
        norm = top + jnp.log(total)
        delta = weighted / total
        finals[0][0:1, :] = norm
        finals[0][1:2, :] = delta
        rows = []
        for value in (norm, delta):
            for _ in range(3):
                part = value.astype(jnp.bfloat16).astype(jnp.float32)
                value = value - part
                rows += [part[:, j * HD : (j + 1) * HD] for j in range(TOK // HD)]
        rows.append(jnp.zeros((STAT_ROWS - len(rows), HD), jnp.float32))
        pack = finals[1]
        pack[0:TOK, :] = q_ref[...]
        pack[TOK : 2 * TOK, :] = g_ref[...]
        pack[2 * TOK :, :] = jnp.concatenate(rows, axis=0).astype(jnp.bfloat16)


def unpacked(rows):
    rows = rows.astype(jnp.float32)
    values = []
    for stat in range(2):
        lanes = []
        for j in range(TOK // HD):
            at = [9 * stat + 3 * part + j for part in range(3)]
            hi, mid, low = [rows[r : r + 1, :] for r in at]
            lanes.append(hi + (mid + low))
        values.append(jnp.concatenate(lanes, axis=1))
    return values


def query_kernel(scale, live, stat_ref, q_ref, g_ref, own_ref, mate_ref, far_ref, out_ref, acc, low):
    acc[...] = jnp.zeros_like(acc)
    norm = stat_ref[0:1, :]
    delta = stat_ref[1:2, :]
    for group, kv_ref in enumerate((own_ref, mate_ref, far_ref)):

        def visit(slot, carry, group=group, kv_ref=kv_ref):
            @pl.when(live[group * SLOTS + slot] != 0)
            def _():
                for part in range(TOK // CHUNK):
                    rows = pl.ds(part * CHUNK, CHUNK)
                    logit = dot(kv_ref[slot, 0, rows, :], q_ref[...], NT) * scale
                    prob = jnp.exp(logit - norm)
                    grad_prob = dot(kv_ref[slot, 1, rows, :], g_ref[...], NT)
                    low[rows, :] = (prob * (grad_prob - delta)).astype(jnp.bfloat16)
                acc[...] += dot(kv_ref[slot, 0], low[...], TN)

            return carry

        lax.fori_loop(0, SLOTS, visit, 0)
    out_ref[...] = (acc[...].T * scale).astype(jnp.bfloat16)


def key_kernel(scale, last, live, k_ref, v_ref, *refs):
    if last:
        qg_ref, stat_ref, acc_in, dk_out, dv_out, acc, prob_low, grad_low = refs
    else:
        qg_ref, acc_in, acc, prob_low, grad_low = refs
    acc[...] = acc_in[...]

    def visit(slot, carry):
        @pl.when(live[slot] != 0)
        def _():
            if last:
                query, grad = qg_ref.at[slot, 0], qg_ref.at[slot, 1]
                norm, delta = unpacked(stat_ref[slot])
            else:
                query = qg_ref.at[slot, pl.ds(0, TOK)]
                grad = qg_ref.at[slot, pl.ds(TOK, TOK)]
                norm, delta = unpacked(qg_ref[slot, pl.ds(2 * TOK, STAT_ROWS), :])
            for part in range(TOK // CHUNK):
                rows = pl.ds(part * CHUNK, CHUNK)
                logit = dot(k_ref[rows, :], query[...], NT) * scale
                prob = jnp.exp(logit - norm)
                grad_prob = dot(v_ref[rows, :], grad[...], NT)
                prob_low[rows, :] = prob.astype(jnp.bfloat16)
                grad_low[rows, :] = (prob * (grad_prob - delta)).astype(jnp.bfloat16)
            acc[0] += dot(grad_low[...], query[...], NN)
            acc[1] += dot(prob_low[...], grad[...], NN)

        return carry

    lax.fori_loop(0, SLOTS, visit, 0)
    if last:
        dk_out[...] = (acc[0] * scale).astype(jnp.bfloat16)
        dv_out[...] = acc[1].astype(jnp.bfloat16)


SMEM = pl.BlockSpec(memory_space=pltpu.SMEM)
VMEM = pl.BlockSpec(memory_space=pltpu.VMEM)


def params():
    return pltpu.CompilerParams(vmem_limit_bytes=40 * 1024 * 1024)


def cost(pairs, matmuls):
    return pl.CostEstimate(
        flops=pairs * matmuls * 2 * TOK * TOK * HD,
        transcendentals=pairs * TOK * TOK,
        bytes_accessed=pairs * 4 * TOK * HD * 2,
    )


def run_stats(scale, live, q, g, kv, state, last):
    state_shape = jax.ShapeDtypeStruct((3, 8, TOK), jnp.float32)
    stat_shape = jax.ShapeDtypeStruct((2, TOK), jnp.float32)
    pack_shape = jax.ShapeDtypeStruct((PACK, HD), jnp.bfloat16)

    def body(*refs):
        stats_kernel(scale, last, *refs)

    return pl.pallas_call(
        body,
        out_shape=(state_shape, stat_shape, pack_shape) if last else (state_shape,),
        in_specs=[SMEM, VMEM, VMEM, VMEM, VMEM],
        out_specs=(VMEM,) * 3 if last else (VMEM,),
        compiler_params=params(),
        cost_estimate=cost(SLOTS, 2),
        name="row_stats",
    )(live, q, g, kv, state)


def run_query(scale, live, stat, q, g, groups):
    def body(*refs):
        query_kernel(scale, *refs)

    return pl.pallas_call(
        body,
        out_shape=jax.ShapeDtypeStruct((TOK, HD), jnp.bfloat16),
        in_specs=[SMEM] + [VMEM] * 6,
        out_specs=VMEM,
        scratch_shapes=[
            pltpu.VMEM((HD, TOK), jnp.float32),
            pltpu.VMEM((TOK, TOK), jnp.bfloat16),
        ],
        compiler_params=params(),
        cost_estimate=cost(3 * SLOTS, 3),
        name="grad_query",
    )(live, stat, q, g, *groups)


def run_key(scale, live, k, v, given, acc, last):
    acc_shape = jax.ShapeDtypeStruct((2, TOK, HD), jnp.float32)
    low_shape = jax.ShapeDtypeStruct((TOK, HD), jnp.bfloat16)

    def body(*refs):
        key_kernel(scale, last, *refs)

    return pl.pallas_call(
        body,
        out_shape=(low_shape, low_shape, acc_shape) if last else (acc_shape,),
        in_specs=[SMEM] + [VMEM] * (3 + len(given)),
        out_specs=(VMEM, VMEM, VMEM) if last else (VMEM,),
        scratch_shapes=[
            pltpu.VMEM((TOK, TOK), jnp.bfloat16),
            pltpu.VMEM((TOK, TOK), jnp.bfloat16),
        ],
        compiler_params=params(),
        cost_estimate=cost(SLOTS, 4),
        name="grad_key",
    )(live, k, v, *given, acc)


def live_slots(key_tiles, tile_count, my_lat, my_z, my_y):
    columns, real = slot_columns(my_z, my_y)
    far_lat = jnp.where(my_lat % 2 == 1, my_lat + 1, my_lat - 1)
    bands = jnp.stack([my_lat, my_lat ^ 1, far_lat])
    band_real = (bands >= 0) & (bands < LAT)
    ids = (bands[:, None] * LON + columns[None, :]).reshape(-1)
    slot_real = (band_real[:, None] & real[None, :]).reshape(-1)
    table = key_tiles.reshape(LAT * LON, -1)
    totals = tile_count.reshape(-1)
    places = jnp.arange(table.shape[1], dtype=jnp.int32)
    own_id = my_lat * LON + my_z * Y + my_y
    own_list = lax.dynamic_index_in_dim(table, own_id, 0, keepdims=False)
    own_total = lax.dynamic_index_in_dim(totals, own_id, 0, keepdims=False)
    i_list = jnp.any(
        (own_list[None, :] == ids[:, None]) & (places < own_total)[None, :], axis=1
    )
    safe = jnp.clip(ids, 0, LAT * LON - 1)
    lists_me = jnp.any(
        (table[safe] == own_id) & (places[None, :] < totals[safe][:, None]), axis=1
    )
    live_keys = (i_list & slot_real).astype(jnp.int32)
    live_queries = (lists_me & slot_real).astype(jnp.int32)
    return live_keys.reshape(3, SLOTS), live_queries.reshape(3, SLOTS)


def per_device(queries, keys, values, cotangent, key_tiles, tile_count):
    scale = HD ** (-0.5)
    my_lat = lax.axis_index("lat")
    my_lon = lax.axis_index("lon")
    my_z, my_y = my_lon // Y, my_lon % Y
    q = queries.reshape(TOK, HD)
    k = keys.reshape(TOK, HD)
    v = values.reshape(TOK, HD)
    g = cotangent.reshape(TOK, HD)

    place = lax.optimization_barrier((my_lat, my_z, my_y))
    live_k, live_q = live_slots(key_tiles, tile_count, *place)

    kv = lax.optimization_barrier(jnp.stack([k, v]))
    qg = jnp.stack([q, g])
    qg = lax.optimization_barrier(qg)
    far_kv = permuted(kv, cross_rule)
    own_kv = spread_own(kv, my_y)
    far_kvs = spread_far(kv, far_kv, my_z, my_y)
    mate_kv = permuted(own_kv, swap_rule)
    far_qg = permuted(qg, cross_rule)
    far_qgs = spread_far(qg, far_qg, my_z, my_y)

    blank = jnp.zeros((8, TOK), jnp.float32)
    state = jnp.stack([blank + NEG_BIG, blank, blank])
    (state,) = run_stats(scale, live_k[0], q, g, own_kv, state, False)
    (state,) = run_stats(scale, live_k[1], q, g, mate_kv, state, False)
    _, stat, pack = run_stats(scale, live_k[2], q, g, far_kvs, state, True)

    own_qg = spread_own(pack, my_y)
    mate_qg = permuted(own_qg, swap_rule)
    far_stats = permuted(own_qg[:, 2 * TOK :], cross_rule)
    grad_query = run_query(
        scale, live_k.reshape(-1), stat, q, g, (own_kv, mate_kv, far_kvs)
    )

    acc = jnp.zeros((2, TOK, HD), jnp.float32)
    (acc,) = run_key(scale, live_q[0], k, v, (own_qg,), acc, False)
    (acc,) = run_key(scale, live_q[1], k, v, (mate_qg,), acc, False)
    grad_key, grad_value, _ = run_key(
        scale, live_q[2], k, v, (far_qgs, far_stats), acc, True
    )
    out_shape = (1, 1, TOK, HD)
    return (
        grad_query.reshape(out_shape),
        grad_key.reshape(out_shape),
        grad_value.reshape(out_shape),
    )


def solution(mesh):
    tile = P("lat", "lon", None, None)

    return jax.shard_map(
        per_device,
        mesh=mesh,
        in_specs=(tile, tile, tile, tile, P(), P()),
        out_specs=(tile, tile, tile),
        check_vma=False,
    )
```

```python
import jax
import jax.numpy as jnp
from jax import lax
from jax.experimental import pallas as pl
from jax.experimental.pallas import tpu as pltpu
from jax.sharding import PartitionSpec as P


Y = 4
ZL = 8
LON = 32
LAT = 16
TOK = 384
HD = 128
SLOTS = 8
NEG_BIG = -1e30
AXES = ("lon", "lat")
CHUNK = 128
STAT_ROWS = 32
PACK = 2 * TOK + STAT_ROWS


SMEM = pl.BlockSpec(memory_space=pltpu.SMEM)
VMEM = pl.BlockSpec(memory_space=pltpu.VMEM)


def cross_of(lat):
    other = lat + 1 if lat % 2 else lat - 1
    return other if 0 <= other < LAT else None


def pairs_of(rule):
    pairs = []
    for lon in range(LON):
        for lat in range(LAT):
            to = rule(lon // Y, lon % Y, lat)
            if to is not None:
                z, y, band = to
                pairs.append((lon * LAT + lat, (z * Y + y) * LAT + band))
    return pairs


def swap_rule(z, y, lat):
    return (z, y, lat ^ 1)


def cross_rule(z, y, lat):
    other = cross_of(lat)
    return None if other is None else (z, y, other)


def z_rule(step):
    unused = 0 if step > 0 else Y - 1

    def rule(z, y, lat):
        return None if y == unused else ((z + step) % ZL, y, lat)

    return rule


def far_z_rule(step):
    unused = 0 if step > 0 else Y - 1

    def rule(z, y, lat):
        if y == unused:
            return None
        if 0 <= z + step < ZL:
            return (z + step, y, lat)
        other = cross_of(lat)
        return None if other is None else ((z + step) % ZL, y, other)

    return rule


def permuted(x, rule):
    return lax.ppermute(x, AXES, pairs_of(rule))


def pack_kernel(my_y, here, before, after, out):
    for peer in range(Y):
        out[peer, 0] = here[...]

        @pl.when(peer < my_y[0])
        def _():
            out[peer, 1] = before[...]

        @pl.when(peer >= my_y[0])
        def _():
            out[peer, 1] = after[...]


def run_pack(my_y, here, before, after):
    return pl.pallas_call(
        pack_kernel,
        out_shape=jax.ShapeDtypeStruct((Y, 2) + here.shape, here.dtype),
        in_specs=[SMEM] + [VMEM] * 3,
        out_specs=VMEM,
        name="pack",
    )(my_y.reshape(1), here, before, after)


def spread_y(here, before, after, my_y):
    groups = [[z * Y + y for y in range(Y)] for z in range(ZL)]
    payload = run_pack(my_y, here, before, after)
    got = lax.all_to_all(
        payload, "lon", 0, 0, axis_index_groups=groups, tiled=True
    )
    return got.reshape((SLOTS,) + here.shape)


def spread_own(here, my_y):
    before = permuted(here, z_rule(1))
    after = permuted(here, z_rule(-1))
    return spread_y(here, before, after, my_y)


def spread_far(here, far, my_z, my_y):
    before = permuted(jnp.where(my_z == ZL - 1, here, far), far_z_rule(1))
    after = permuted(jnp.where(my_z == 0, here, far), far_z_rule(-1))
    return spread_y(far, before, after, my_y)


def slot_columns(my_z, my_y):
    sender = jnp.arange(Y, dtype=jnp.int32)
    near = my_z * Y + sender
    beside = (my_z + jnp.where(sender > my_y, -1, 1)) % ZL * Y + sender
    columns = jnp.stack([near, beside], axis=1).reshape(SLOTS)
    real = jnp.stack([sender >= 0, sender != my_y], axis=1).reshape(SLOTS)
    return columns, real


NT = (((1,), (1,)), ((), ()))
NN = (((1,), (0,)), ((), ()))
TN = (((0,), (0,)), ((), ()))


def dot(a, b, dims):
    return lax.dot_general(a, b, dims, preferred_element_type=jnp.float32)


def stats_kernel(scale, last, live, q_ref, g_ref, kv_ref, st_in, st_out, *finals):
    st_out[...] = st_in[...]

    def visit(slot, carry):
        @pl.when(live[slot] != 0)
        def _():
            for part in range(TOK // CHUNK):
                rows = pl.ds(part * CHUNK, CHUNK)
                logit = dot(kv_ref[slot, 0, rows, :], q_ref[...], NT) * scale
                grad_prob = dot(kv_ref[slot, 1, rows, :], g_ref[...], NT)
                logit = logit.reshape(CHUNK // 8, 8, TOK)
                grad_prob = grad_prob.reshape(CHUNK // 8, 8, TOK)
                old_max = st_out[0]
                new_max = jnp.maximum(old_max, jnp.max(logit, axis=0))
                rescale = jnp.exp(old_max - new_max)
                power = jnp.exp(logit - new_max[None])
                st_out[0] = new_max
                st_out[1] = st_out[1] * rescale + jnp.sum(power, axis=0)
                st_out[2] = st_out[2] * rescale + jnp.sum(power * grad_prob, axis=0)

        return carry

    lax.fori_loop(0, SLOTS, visit, 0)
    if last:
        top = jnp.max(st_out[0], axis=0, keepdims=True)
        weight = jnp.exp(st_out[0] - top)
        total = jnp.sum(st_out[1] * weight, axis=0, keepdims=True)
        weighted = jnp.sum(st_out[2] * weight, axis=0, keepdims=True)
        norm = top + jnp.log(total)
        delta = weighted / total
        finals[0][0:1, :] = norm
        finals[0][1:2, :] = delta
        rows = []
        for value in (norm, delta):
            for _ in range(3):
                part = value.astype(jnp.bfloat16).astype(jnp.float32)
                value = value - part
                rows += [part[:, j * HD : (j + 1) * HD] for j in range(TOK // HD)]
        rows.append(jnp.zeros((STAT_ROWS - len(rows), HD), jnp.float32))
        pack = finals[1]
        pack[0:TOK, :] = q_ref[...]
        pack[TOK : 2 * TOK, :] = g_ref[...]
        pack[2 * TOK :, :] = jnp.concatenate(rows, axis=0).astype(jnp.bfloat16)


def unpacked(rows):
    rows = rows.astype(jnp.float32)
    values = []
    for stat in range(2):
        lanes = []
        for j in range(TOK // HD):
            at = [9 * stat + 3 * part + j for part in range(3)]
            hi, mid, low = [rows[r : r + 1, :] for r in at]
            lanes.append(hi + (mid + low))
        values.append(jnp.concatenate(lanes, axis=1))
    return values


def query_kernel(scale, live, stat_ref, q_ref, g_ref, own_ref, mate_ref, far_ref, out_ref, acc, low):
    acc[...] = jnp.zeros_like(acc)
    norm = stat_ref[0:1, :]
    delta = stat_ref[1:2, :]
    for group, kv_ref in enumerate((own_ref, mate_ref, far_ref)):

        def visit(slot, carry, group=group, kv_ref=kv_ref):
            @pl.when(live[group * SLOTS + slot] != 0)
            def _():
                for part in range(TOK // CHUNK):
                    rows = pl.ds(part * CHUNK, CHUNK)
                    logit = dot(kv_ref[slot, 0, rows, :], q_ref[...], NT) * scale
                    prob = jnp.exp(logit - norm)
                    grad_prob = dot(kv_ref[slot, 1, rows, :], g_ref[...], NT)
                    low[rows, :] = (prob * (grad_prob - delta)).astype(jnp.bfloat16)
                acc[...] += dot(kv_ref[slot, 0], low[...], TN)

            return carry

        lax.fori_loop(0, SLOTS, visit, 0)
    out_ref[...] = (acc[...].T * scale).astype(jnp.bfloat16)


def key_kernel(scale, last, live, k_ref, v_ref, *refs):
    if last:
        qg_ref, stat_ref, acc_in, dk_out, dv_out, acc, prob_low, grad_low = refs
    else:
        qg_ref, acc_in, acc, prob_low, grad_low = refs
    acc[...] = acc_in[...]

    def visit(slot, carry):
        @pl.when(live[slot] != 0)
        def _():
            if last:
                query, grad = qg_ref.at[slot, 0], qg_ref.at[slot, 1]
                norm, delta = unpacked(stat_ref[slot])
            else:
                query = qg_ref.at[slot, pl.ds(0, TOK)]
                grad = qg_ref.at[slot, pl.ds(TOK, TOK)]
                norm, delta = unpacked(qg_ref[slot, pl.ds(2 * TOK, STAT_ROWS), :])
            for part in range(TOK // CHUNK):
                rows = pl.ds(part * CHUNK, CHUNK)
                logit = dot(k_ref[rows, :], query[...], NT) * scale
                prob = jnp.exp(logit - norm)
                grad_prob = dot(v_ref[rows, :], grad[...], NT)
                prob_low[rows, :] = prob.astype(jnp.bfloat16)
                grad_low[rows, :] = (prob * (grad_prob - delta)).astype(jnp.bfloat16)
            acc[0] += dot(grad_low[...], query[...], NN)
            acc[1] += dot(prob_low[...], grad[...], NN)

        return carry

    lax.fori_loop(0, SLOTS, visit, 0)
    if last:
        dk_out[...] = (acc[0] * scale).astype(jnp.bfloat16)
        dv_out[...] = acc[1].astype(jnp.bfloat16)


def params():
    return pltpu.CompilerParams(vmem_limit_bytes=40 * 1024 * 1024)


def cost(pairs, matmuls):
    return pl.CostEstimate(
        flops=pairs * matmuls * 2 * TOK * TOK * HD,
        transcendentals=pairs * TOK * TOK,
        bytes_accessed=pairs * 4 * TOK * HD * 2,
    )


def run_stats(scale, live, q, g, kv, state, last):
    state_shape = jax.ShapeDtypeStruct((3, 8, TOK), jnp.float32)
    stat_shape = jax.ShapeDtypeStruct((2, TOK), jnp.float32)
    pack_shape = jax.ShapeDtypeStruct((PACK, HD), jnp.bfloat16)

    def body(*refs):
        stats_kernel(scale, last, *refs)

    return pl.pallas_call(
        body,
        out_shape=(state_shape, stat_shape, pack_shape) if last else (state_shape,),
        in_specs=[SMEM, VMEM, VMEM, VMEM, VMEM],
        out_specs=(VMEM,) * 3 if last else (VMEM,),
        compiler_params=params(),
        cost_estimate=cost(SLOTS, 2),
        name="row_stats",
    )(live, q, g, kv, state)


def run_query(scale, live, stat, q, g, groups):
    def body(*refs):
        query_kernel(scale, *refs)

    return pl.pallas_call(
        body,
        out_shape=jax.ShapeDtypeStruct((TOK, HD), jnp.bfloat16),
        in_specs=[SMEM] + [VMEM] * 6,
        out_specs=VMEM,
        scratch_shapes=[
            pltpu.VMEM((HD, TOK), jnp.float32),
            pltpu.VMEM((TOK, TOK), jnp.bfloat16),
        ],
        compiler_params=params(),
        cost_estimate=cost(3 * SLOTS, 3),
        name="grad_query",
    )(live, stat, q, g, *groups)


def run_key(scale, live, k, v, given, acc, last):
    acc_shape = jax.ShapeDtypeStruct((2, TOK, HD), jnp.float32)
    low_shape = jax.ShapeDtypeStruct((TOK, HD), jnp.bfloat16)

    def body(*refs):
        key_kernel(scale, last, *refs)

    return pl.pallas_call(
        body,
        out_shape=(low_shape, low_shape, acc_shape) if last else (acc_shape,),
        in_specs=[SMEM] + [VMEM] * (3 + len(given)),
        out_specs=(VMEM, VMEM, VMEM) if last else (VMEM,),
        scratch_shapes=[
            pltpu.VMEM((TOK, TOK), jnp.bfloat16),
            pltpu.VMEM((TOK, TOK), jnp.bfloat16),
        ],
        compiler_params=params(),
        cost_estimate=cost(SLOTS, 4),
        name="grad_key",
    )(live, k, v, *given, acc)


def live_slots(key_tiles, tile_count, my_lat, my_z, my_y):
    columns, real = slot_columns(my_z, my_y)
    far_lat = jnp.where(my_lat % 2 == 1, my_lat + 1, my_lat - 1)
    bands = jnp.stack([my_lat, my_lat ^ 1, far_lat])
    band_real = (bands >= 0) & (bands < LAT)
    ids = (bands[:, None] * LON + columns[None, :]).reshape(-1)
    slot_real = (band_real[:, None] & real[None, :]).reshape(-1)
    table = key_tiles.reshape(LAT * LON, -1)
    totals = tile_count.reshape(-1)
    places = jnp.arange(table.shape[1], dtype=jnp.int32)
    own_id = my_lat * LON + my_z * Y + my_y
    own_list = lax.dynamic_index_in_dim(table, own_id, 0, keepdims=False)
    own_total = lax.dynamic_index_in_dim(totals, own_id, 0, keepdims=False)
    i_list = jnp.any(
        (own_list[None, :] == ids[:, None]) & (places < own_total)[None, :], axis=1
    )
    safe = jnp.clip(ids, 0, LAT * LON - 1)
    lists_me = jnp.any(
        (table[safe] == own_id) & (places[None, :] < totals[safe][:, None]), axis=1
    )
    live_keys = (i_list & slot_real).astype(jnp.int32)
    live_queries = (lists_me & slot_real).astype(jnp.int32)
    return live_keys.reshape(3, SLOTS), live_queries.reshape(3, SLOTS)


def per_device(queries, keys, values, cotangent, key_tiles, tile_count):
    scale = HD ** (-0.5)
    my_lat = lax.axis_index("lat")
    my_lon = lax.axis_index("lon")
    my_z, my_y = my_lon // Y, my_lon % Y
    q = queries.reshape(TOK, HD)
    k = keys.reshape(TOK, HD)
    v = values.reshape(TOK, HD)
    g = cotangent.reshape(TOK, HD)

    place = lax.optimization_barrier((my_lat, my_z, my_y))
    live_k, live_q = live_slots(key_tiles, tile_count, *place)

    kv = lax.optimization_barrier(jnp.stack([k, v]))
    qg = jnp.stack([q, g])
    qg = lax.optimization_barrier(qg)
    far_kv = permuted(kv, cross_rule)
    own_kv = spread_own(kv, my_y)
    far_kvs = spread_far(kv, far_kv, my_z, my_y)
    mate_kv = permuted(own_kv, swap_rule)
    far_qg = permuted(qg, cross_rule)
    far_qgs = spread_far(qg, far_qg, my_z, my_y)

    blank = jnp.zeros((8, TOK), jnp.float32)
    state = jnp.stack([blank + NEG_BIG, blank, blank])
    (state,) = run_stats(scale, live_k[0], q, g, own_kv, state, False)
    (state,) = run_stats(scale, live_k[1], q, g, mate_kv, state, False)
    _, stat, pack = run_stats(scale, live_k[2], q, g, far_kvs, state, True)

    own_qg = spread_own(pack, my_y)
    mate_qg = permuted(own_qg, swap_rule)
    far_stats = permuted(own_qg[:, 2 * TOK :], cross_rule)
    grad_query = run_query(
        scale, live_k.reshape(-1), stat, q, g, (own_kv, mate_kv, far_kvs)
    )

    acc = jnp.zeros((2, TOK, HD), jnp.float32)
    (acc,) = run_key(scale, live_q[0], k, v, (own_qg,), acc, False)
    (acc,) = run_key(scale, live_q[1], k, v, (mate_qg,), acc, False)
    grad_key, grad_value, _ = run_key(
        scale, live_q[2], k, v, (far_qgs, far_stats), acc, True
    )
    out_shape = (1, 1, TOK, HD)
    return (
        grad_query.reshape(out_shape),
        grad_key.reshape(out_shape),
        grad_value.reshape(out_shape),
    )


def solution(mesh):
    tile = P("lat", "lon", None, None)

    return jax.shard_map(
        per_device,
        mesh=mesh,
        in_specs=(tile, tile, tile, tile, P(), P()),
        out_specs=(tile, tile, tile),
        check_vma=False,
    )
```

```python
import jax
import jax.numpy as jnp
from jax import lax
from jax.experimental import pallas as pl
from jax.experimental.pallas import tpu as pltpu
from jax.sharding import PartitionSpec as P


Y = 4
ZL = 8
LON = 32
LAT = 16
TOK = 384
HD = 128
SLOTS = 8
NEG_BIG = -1e30
AXES = ("lon", "lat")
WIDTHS = (7, 3, 1)
STAT_WIDTHS = (2, 1)
MOST = max(WIDTHS)
LOG2_E = 1.4426950408889634
STAT_ROWS = 32
PACK = 2 * TOK + STAT_ROWS


SMEM = pl.BlockSpec(memory_space=pltpu.SMEM)
VMEM = pl.BlockSpec(memory_space=pltpu.VMEM)


def cross_of(lat):
    other = lat + 1 if lat % 2 else lat - 1
    return other if 0 <= other < LAT else None


def pairs_of(rule):
    pairs = []
    for lon in range(LON):
        for lat in range(LAT):
            to = rule(lon // Y, lon % Y, lat)
            if to is not None:
                z, y, band = to
                pairs.append((lon * LAT + lat, (z * Y + y) * LAT + band))
    return pairs


def swap_rule(z, y, lat):
    return (z, y, lat ^ 1)


def cross_rule(z, y, lat):
    other = cross_of(lat)
    return None if other is None else (z, y, other)


def z_rule(step):
    unused = 0 if step > 0 else Y - 1

    def rule(z, y, lat):
        return None if y == unused else ((z + step) % ZL, y, lat)

    return rule


def far_z_rule(step):
    unused = 0 if step > 0 else Y - 1

    def rule(z, y, lat):
        if y == unused:
            return None
        if 0 <= z + step < ZL:
            return (z + step, y, lat)
        other = cross_of(lat)
        return None if other is None else ((z + step) % ZL, y, other)

    return rule


def permuted(x, rule):
    return lax.ppermute(x, AXES, pairs_of(rule))


def pack_kernel(my_y, here, before, after, out):
    for peer in range(Y):
        out[peer, 0] = here[...]

        @pl.when(peer < my_y[0])
        def _():
            out[peer, 1] = before[...]

        @pl.when(peer >= my_y[0])
        def _():
            out[peer, 1] = after[...]


def run_pack(my_y, here, before, after):
    return pl.pallas_call(
        pack_kernel,
        out_shape=jax.ShapeDtypeStruct((Y, 2) + here.shape, here.dtype),
        in_specs=[SMEM] + [VMEM] * 3,
        out_specs=VMEM,
        name="pack",
    )(my_y.reshape(1), here, before, after)


def spread_y(here, before, after, my_y):
    groups = [[z * Y + y for y in range(Y)] for z in range(ZL)]
    payload = run_pack(my_y, here, before, after)
    got = lax.all_to_all(
        payload, "lon", 0, 0, axis_index_groups=groups, tiled=True
    )
    return got.reshape((SLOTS,) + here.shape)


def spread_own(here, my_y):
    before = permuted(here, z_rule(1))
    after = permuted(here, z_rule(-1))
    return spread_y(here, before, after, my_y)


def spread_far(here, far, my_z, my_y):
    before = permuted(jnp.where(my_z == ZL - 1, here, far), far_z_rule(1))
    after = permuted(jnp.where(my_z == 0, here, far), far_z_rule(-1))
    return spread_y(far, before, after, my_y)


def slot_columns(my_z, my_y):
    sender = jnp.arange(Y, dtype=jnp.int32)
    near = my_z * Y + sender
    beside = (my_z + jnp.where(sender > my_y, -1, 1)) % ZL * Y + sender
    columns = jnp.stack([near, beside], axis=1).reshape(SLOTS)
    real = jnp.stack([sender >= 0, sender != my_y], axis=1).reshape(SLOTS)
    return columns, real


NT = (((1,), (1,)), ((), ()))
NN = (((1,), (0,)), ((), ()))
TN = (((0,), (0,)), ((), ()))


def dot(a, b, dims):
    return lax.dot_general(a, b, dims, preferred_element_type=jnp.float32)


def each_live(live, base, order, visit, widths):
    order[SLOTS] = 0
    for slot in range(SLOTS):

        @pl.when(live[base + slot] != 0)
        def _(slot=slot):
            count = order[SLOTS]
            order[count] = slot
            order[SLOTS] = count + 1

    count = order[SLOTS]
    start = 0
    for width in widths:
        rounds = (count - start) // width

        def several(i, carry, width=width, start=start):
            visit([order[start + i * width + j] for j in range(width)])
            return carry

        lax.fori_loop(0, rounds, several, 0)
        start = start + rounds * width


def stats_kernel(scale, last, live, q_ref, g_ref, kv_ref, st_in, st_out, *rest):
    finals, order = rest[:-1], rest[-1]
    st_out[...] = st_in[...]

    def visit(slots):
        logits, grad_probs = [], []
        for slot in slots:
            logits.append(dot(kv_ref[slot, 0], q_ref[...], NT) * (scale * LOG2_E))
            grad_probs.append(dot(kv_ref[slot, 1], g_ref[...], NT))
        logits = [x.reshape(TOK // 8, 8, TOK) for x in logits]
        grad_probs = [x.reshape(TOK // 8, 8, TOK) for x in grad_probs]
        old_max = new_max = st_out[0]
        for logit in logits:
            new_max = jnp.maximum(new_max, jnp.max(logit, axis=0))
        rescale = jnp.exp2(old_max - new_max)
        total = st_out[1] * rescale
        weighted = st_out[2] * rescale
        for logit, grad_prob in zip(logits, grad_probs):
            power = jnp.exp2(logit - new_max[None])
            total += jnp.sum(power, axis=0)
            weighted += jnp.sum(power * grad_prob, axis=0)
        st_out[0] = new_max
        st_out[1] = total
        st_out[2] = weighted

    each_live(live, 0, order, visit, STAT_WIDTHS)
    if last:
        top = jnp.max(st_out[0], axis=0, keepdims=True)
        weight = jnp.exp2(st_out[0] - top)
        total = jnp.sum(st_out[1] * weight, axis=0, keepdims=True)
        weighted = jnp.sum(st_out[2] * weight, axis=0, keepdims=True)
        norm = top + jnp.log(total) * LOG2_E
        delta = weighted / total
        finals[0][0:1, :] = norm
        finals[0][1:2, :] = delta
        rows = []
        for value in (norm, delta):
            for _ in range(3):
                part = value.astype(jnp.bfloat16).astype(jnp.float32)
                value = value - part
                rows += [part[:, j * HD : (j + 1) * HD] for j in range(TOK // HD)]
        rows.append(jnp.zeros((STAT_ROWS - len(rows), HD), jnp.float32))
        pack = finals[1]
        pack[0:TOK, :] = q_ref[...]
        pack[TOK : 2 * TOK, :] = g_ref[...]
        pack[2 * TOK :, :] = jnp.concatenate(rows, axis=0).astype(jnp.bfloat16)


def unpacked(rows):
    rows = rows.astype(jnp.float32)
    values = []
    for stat in range(2):
        lanes = []
        for j in range(TOK // HD):
            at = [9 * stat + 3 * part + j for part in range(3)]
            hi, mid, low = [rows[r : r + 1, :] for r in at]
            lanes.append(hi + (mid + low))
        values.append(jnp.concatenate(lanes, axis=1))
    return values


def query_kernel(scale, live, stat_ref, q_ref, g_ref, own_ref, mate_ref, far_ref, out_ref, acc, low, order):
    acc[...] = jnp.zeros_like(acc)
    norm = stat_ref[0:1, :]
    delta = stat_ref[1:2, :]
    for group, kv_ref in enumerate((own_ref, mate_ref, far_ref)):

        def visit(slots, kv_ref=kv_ref):
            for i, slot in enumerate(slots):
                logit = dot(kv_ref[slot, 0], q_ref[...], NT) * (scale * LOG2_E)
                prob = jnp.exp2(logit - norm)
                grad_prob = dot(kv_ref[slot, 1], g_ref[...], NT)
                low[i] = (prob * (grad_prob - delta)).astype(jnp.bfloat16)
            acc[...] += sum(
                dot(kv_ref[slot, 0], low[i], TN) for i, slot in enumerate(slots)
            )

        each_live(live, group * SLOTS, order, visit, WIDTHS)
    out_ref[...] = (acc[...].T * scale).astype(jnp.bfloat16)


def key_kernel(scale, last, live, k_ref, v_ref, *refs):
    refs, (prob_low, grad_low, order) = refs[:-3], refs[-3:]
    if last:
        qg_ref, stat_ref, acc_in, dk_out, dv_out, acc = refs
    else:
        qg_ref, acc_in, acc = refs
    acc[...] = acc_in[...]

    def visit(slots):
        queries, grads = [], []
        for i, slot in enumerate(slots):
            if last:
                query, grad = qg_ref[slot, 0], qg_ref[slot, 1]
                norm, delta = unpacked(stat_ref[slot])
            else:
                query = qg_ref[slot, pl.ds(0, TOK)]
                grad = qg_ref[slot, pl.ds(TOK, TOK)]
                norm, delta = unpacked(qg_ref[slot, pl.ds(2 * TOK, STAT_ROWS), :])
            logit = dot(k_ref[...], query, NT) * (scale * LOG2_E)
            prob = jnp.exp2(logit - norm)
            grad_prob = dot(v_ref[...], grad, NT)
            prob_low[i] = prob.astype(jnp.bfloat16)
            grad_low[i] = (prob * (grad_prob - delta)).astype(jnp.bfloat16)
            queries.append(query)
            grads.append(grad)
        acc[0] += sum(dot(grad_low[i], x, NN) for i, x in enumerate(queries))
        acc[1] += sum(dot(prob_low[i], x, NN) for i, x in enumerate(grads))

    each_live(live, 0, order, visit, WIDTHS)
    if last:
        dk_out[...] = (acc[0] * scale).astype(jnp.bfloat16)
        dv_out[...] = acc[1].astype(jnp.bfloat16)


def params():
    return pltpu.CompilerParams(vmem_limit_bytes=40 * 1024 * 1024)


def cost(pairs, matmuls):
    return pl.CostEstimate(
        flops=pairs * matmuls * 2 * TOK * TOK * HD,
        transcendentals=pairs * TOK * TOK,
        bytes_accessed=pairs * 4 * TOK * HD * 2,
    )


def run_stats(scale, live, q, g, kv, state, last):
    state_shape = jax.ShapeDtypeStruct((3, 8, TOK), jnp.float32)
    stat_shape = jax.ShapeDtypeStruct((2, TOK), jnp.float32)
    pack_shape = jax.ShapeDtypeStruct((PACK, HD), jnp.bfloat16)

    def body(*refs):
        stats_kernel(scale, last, *refs)

    return pl.pallas_call(
        body,
        out_shape=(state_shape, stat_shape, pack_shape) if last else (state_shape,),
        in_specs=[SMEM, VMEM, VMEM, VMEM, VMEM],
        out_specs=(VMEM,) * 3 if last else (VMEM,),
        scratch_shapes=[pltpu.SMEM((SLOTS + 1,), jnp.int32)],
        compiler_params=params(),
        cost_estimate=cost(SLOTS, 2),
        name="row_stats",
    )(live, q, g, kv, state)


def run_query(scale, live, stat, q, g, groups):
    def body(*refs):
        query_kernel(scale, *refs)

    return pl.pallas_call(
        body,
        out_shape=jax.ShapeDtypeStruct((TOK, HD), jnp.bfloat16),
        in_specs=[SMEM] + [VMEM] * 6,
        out_specs=VMEM,
        scratch_shapes=[
            pltpu.VMEM((HD, TOK), jnp.float32),
            pltpu.VMEM((MOST, TOK, TOK), jnp.bfloat16),
            pltpu.SMEM((SLOTS + 1,), jnp.int32),
        ],
        compiler_params=params(),
        cost_estimate=cost(3 * SLOTS, 3),
        name="grad_query",
    )(live, stat, q, g, *groups)


def run_key(scale, live, k, v, given, acc, last):
    acc_shape = jax.ShapeDtypeStruct((2, TOK, HD), jnp.float32)
    low_shape = jax.ShapeDtypeStruct((TOK, HD), jnp.bfloat16)

    def body(*refs):
        key_kernel(scale, last, *refs)

    return pl.pallas_call(
        body,
        out_shape=(low_shape, low_shape, acc_shape) if last else (acc_shape,),
        in_specs=[SMEM] + [VMEM] * (3 + len(given)),
        out_specs=(VMEM, VMEM, VMEM) if last else (VMEM,),
        scratch_shapes=[
            pltpu.VMEM((MOST, TOK, TOK), jnp.bfloat16),
            pltpu.VMEM((MOST, TOK, TOK), jnp.bfloat16),
            pltpu.SMEM((SLOTS + 1,), jnp.int32),
        ],
        compiler_params=params(),
        cost_estimate=cost(SLOTS, 4),
        name="grad_key",
    )(live, k, v, *given, acc)


def live_slots(key_tiles, tile_count, my_lat, my_z, my_y):
    columns, real = slot_columns(my_z, my_y)
    far_lat = jnp.where(my_lat % 2 == 1, my_lat + 1, my_lat - 1)
    bands = jnp.stack([my_lat, my_lat ^ 1, far_lat])
    band_real = (bands >= 0) & (bands < LAT)
    ids = (bands[:, None] * LON + columns[None, :]).reshape(-1)
    slot_real = (band_real[:, None] & real[None, :]).reshape(-1)
    table = key_tiles.reshape(LAT * LON, -1)
    totals = tile_count.reshape(-1)
    places = jnp.arange(table.shape[1], dtype=jnp.int32)
    own_id = my_lat * LON + my_z * Y + my_y
    own_list = lax.dynamic_index_in_dim(table, own_id, 0, keepdims=False)
    own_total = lax.dynamic_index_in_dim(totals, own_id, 0, keepdims=False)
    i_list = jnp.any(
        (own_list[None, :] == ids[:, None]) & (places < own_total)[None, :], axis=1
    )
    safe = jnp.clip(ids, 0, LAT * LON - 1)
    lists_me = jnp.any(
        (table[safe] == own_id) & (places[None, :] < totals[safe][:, None]), axis=1
    )
    live_keys = (i_list & slot_real).astype(jnp.int32)
    live_queries = (lists_me & slot_real).astype(jnp.int32)
    return live_keys.reshape(3, SLOTS), live_queries.reshape(3, SLOTS)


def per_device(queries, keys, values, cotangent, key_tiles, tile_count):
    scale = HD ** (-0.5)
    my_lat = lax.axis_index("lat")
    my_lon = lax.axis_index("lon")
    my_z, my_y = my_lon // Y, my_lon % Y
    q = queries.reshape(TOK, HD)
    k = keys.reshape(TOK, HD)
    v = values.reshape(TOK, HD)
    g = cotangent.reshape(TOK, HD)

    place = lax.optimization_barrier((my_lat, my_z, my_y))
    live_k, live_q = live_slots(key_tiles, tile_count, *place)

    kv = lax.optimization_barrier(jnp.stack([k, v]))
    qg = jnp.stack([q, g])
    qg = lax.optimization_barrier(qg)
    far_kv = permuted(kv, cross_rule)
    own_kv = spread_own(kv, my_y)
    far_kvs = spread_far(kv, far_kv, my_z, my_y)
    mate_kv = permuted(own_kv, swap_rule)
    far_qg = permuted(qg, cross_rule)
    far_qgs = spread_far(qg, far_qg, my_z, my_y)

    blank = jnp.zeros((8, TOK), jnp.float32)
    state = jnp.stack([blank + NEG_BIG, blank, blank])
    (state,) = run_stats(scale, live_k[0], q, g, own_kv, state, False)
    (state,) = run_stats(scale, live_k[1], q, g, mate_kv, state, False)
    _, stat, pack = run_stats(scale, live_k[2], q, g, far_kvs, state, True)

    own_qg = spread_own(pack, my_y)
    mate_qg = permuted(own_qg, swap_rule)
    far_stats = permuted(own_qg[:, 2 * TOK :], cross_rule)
    grad_query = run_query(
        scale, live_k.reshape(-1), stat, q, g, (own_kv, mate_kv, far_kvs)
    )

    acc = jnp.zeros((2, TOK, HD), jnp.float32)
    (acc,) = run_key(scale, live_q[0], k, v, (own_qg,), acc, False)
    (acc,) = run_key(scale, live_q[1], k, v, (mate_qg,), acc, False)
    grad_key, grad_value, _ = run_key(
        scale, live_q[2], k, v, (far_qgs, far_stats), acc, True
    )
    out_shape = (1, 1, TOK, HD)
    return (
        grad_query.reshape(out_shape),
        grad_key.reshape(out_shape),
        grad_value.reshape(out_shape),
    )


def solution(mesh):
    tile = P("lat", "lon", None, None)

    return jax.shard_map(
        per_device,
        mesh=mesh,
        in_specs=(tile, tile, tile, tile, P(), P()),
        out_specs=(tile, tile, tile),
        check_vma=False,
    )
```

```python
import jax
import jax.numpy as jnp
from jax import lax
from jax.experimental import pallas as pl
from jax.experimental.pallas import tpu as pltpu
from jax.sharding import PartitionSpec as P


Y = 4
ZL = 8
LON = 32
LAT = 16
TOK = 384
HD = 128
SLOTS = 8
NEG_BIG = -1e30
AXES = ("lon", "lat")
WIDTHS = (7, 3, 1)
STAT_WIDTHS = (2, 1)
MOST = max(WIDTHS)
LOG2_E = 1.4426950408889634
STAT_ROWS = 32
PACK = 2 * TOK + STAT_ROWS


SMEM = pl.BlockSpec(memory_space=pltpu.SMEM)
VMEM = pl.BlockSpec(memory_space=pltpu.VMEM)


def cross_of(lat):
    other = lat + 1 if lat % 2 else lat - 1
    return other if 0 <= other < LAT else None


def pairs_of(rule):
    pairs = []
    for lon in range(LON):
        for lat in range(LAT):
            to = rule(lon // Y, lon % Y, lat)
            if to is not None:
                z, y, band = to
                pairs.append((lon * LAT + lat, (z * Y + y) * LAT + band))
    return pairs


def swap_rule(z, y, lat):
    return (z, y, lat ^ 1)


def cross_rule(z, y, lat):
    other = cross_of(lat)
    return None if other is None else (z, y, other)


def z_rule(step):
    unused = 0 if step > 0 else Y - 1

    def rule(z, y, lat):
        return None if y == unused else ((z + step) % ZL, y, lat)

    return rule


def far_z_rule(step):
    unused = 0 if step > 0 else Y - 1

    def rule(z, y, lat):
        if y == unused:
            return None
        if 0 <= z + step < ZL:
            return (z + step, y, lat)
        other = cross_of(lat)
        return None if other is None else ((z + step) % ZL, y, other)

    return rule


def permuted(x, rule):
    return lax.ppermute(x, AXES, pairs_of(rule))


def pack_kernel(my_y, here, before, after, out):
    rows = pl.ds(0, here.shape[-2])
    lead = (slice(None),) * (len(here.shape) - 2)
    for peer in range(Y):
        out[(peer, 0) + lead + (rows,)] = here[...]

        @pl.when(peer < my_y[0])
        def _():
            out[(peer, 1) + lead + (rows,)] = before[...]

        @pl.when(peer >= my_y[0])
        def _():
            out[(peer, 1) + lead + (rows,)] = after[...]


def run_pack(my_y, here, before, after, height=None):
    piece = here.shape if height is None else (height,) + here.shape[1:]
    return pl.pallas_call(
        pack_kernel,
        out_shape=jax.ShapeDtypeStruct((Y, 2) + piece, here.dtype),
        in_specs=[SMEM] + [VMEM] * 3,
        out_specs=VMEM,
        name="pack",
    )(my_y.reshape(1), here, before, after)


def put_kernel(start, my_y, here, before, after, _, out, sems):
    rows = pl.ds(start, here.shape[0])

    def near(peer):
        return pltpu.make_async_copy(here, out.at[peer, 0, rows], sems.at[2 * peer])

    def beside(peer, source):
        return pltpu.make_async_copy(
            source, out.at[peer, 1, rows], sems.at[2 * peer + 1]
        )

    for peer in range(Y):
        near(peer).start()

        @pl.when(peer < my_y[0])
        def _():
            beside(peer, before).start()

        @pl.when(peer >= my_y[0])
        def _():
            beside(peer, after).start()

    for peer in range(Y):
        near(peer).wait()
        beside(peer, after).wait()


def run_put(my_y, here, before, after, payload):
    anywhere = pl.BlockSpec(memory_space=pl.ANY)

    def body(*refs):
        put_kernel(payload.shape[2] - here.shape[0], *refs)

    return pl.pallas_call(
        body,
        out_shape=jax.ShapeDtypeStruct(payload.shape, payload.dtype),
        in_specs=[SMEM] + [VMEM] * 3 + [anywhere],
        out_specs=anywhere,
        scratch_shapes=[pltpu.SemaphoreType.DMA((2 * Y,))],
        input_output_aliases={4: 0},
        name="put",
    )(my_y.reshape(1), here, before, after, payload)


def exchanged(payload):
    groups = [[z * Y + y for y in range(Y)] for z in range(ZL)]
    got = lax.all_to_all(
        payload, "lon", 0, 0, axis_index_groups=groups, tiled=True
    )
    return got.reshape((SLOTS,) + payload.shape[2:])


def spread_y(here, before, after, my_y):
    payload = run_pack(my_y, here, before, after)
    return exchanged(payload)


def spread_own(here, my_y):
    before = permuted(here, z_rule(1))
    after = permuted(here, z_rule(-1))
    return spread_y(here, before, after, my_y)


def spread_far(here, far, my_z, my_y):
    before = permuted(jnp.where(my_z == ZL - 1, here, far), far_z_rule(1))
    after = permuted(jnp.where(my_z == 0, here, far), far_z_rule(-1))
    return spread_y(far, before, after, my_y)


def slot_columns(my_z, my_y):
    sender = jnp.arange(Y, dtype=jnp.int32)
    near = my_z * Y + sender
    beside = (my_z + jnp.where(sender > my_y, -1, 1)) % ZL * Y + sender
    columns = jnp.stack([near, beside], axis=1).reshape(SLOTS)
    real = jnp.stack([sender >= 0, sender != my_y], axis=1).reshape(SLOTS)
    return columns, real


NT = (((1,), (1,)), ((), ()))
NN = (((1,), (0,)), ((), ()))
TN = (((0,), (0,)), ((), ()))


def dot(a, b, dims):
    return lax.dot_general(a, b, dims, preferred_element_type=jnp.float32)


def each_live(live, base, order, visit, widths):
    order[SLOTS] = 0
    for slot in range(SLOTS):

        @pl.when(live[base + slot] != 0)
        def _(slot=slot):
            count = order[SLOTS]
            order[count] = slot
            order[SLOTS] = count + 1

    count = order[SLOTS]
    start = 0
    for width in widths:
        rounds = (count - start) // width

        def several(i, carry, width=width, start=start):
            visit([order[start + i * width + j] for j in range(width)])
            return carry

        lax.fori_loop(0, rounds, several, 0)
        start = start + rounds * width


def stats_kernel(scale, last, live, q_ref, g_ref, kv_ref, st_in, st_out, *rest):
    finals, order = rest[:-1], rest[-1]
    st_out[...] = st_in[...]

    def visit(slots):
        logits, grad_probs = [], []
        for slot in slots:
            logits.append(dot(kv_ref[slot, 0], q_ref[...], NT) * (scale * LOG2_E))
            grad_probs.append(dot(kv_ref[slot, 1], g_ref[...], NT))
        logits = [x.reshape(TOK // 8, 8, TOK) for x in logits]
        grad_probs = [x.reshape(TOK // 8, 8, TOK) for x in grad_probs]
        old_max = new_max = st_out[0]
        for logit in logits:
            new_max = jnp.maximum(new_max, jnp.max(logit, axis=0))
        rescale = jnp.exp2(old_max - new_max)
        total = st_out[1] * rescale
        weighted = st_out[2] * rescale
        for logit, grad_prob in zip(logits, grad_probs):
            power = jnp.exp2(logit - new_max[None])
            total += jnp.sum(power, axis=0)
            weighted += jnp.sum(power * grad_prob, axis=0)
        st_out[0] = new_max
        st_out[1] = total
        st_out[2] = weighted

    each_live(live, 0, order, visit, STAT_WIDTHS)
    if last:
        top = jnp.max(st_out[0], axis=0, keepdims=True)
        weight = jnp.exp2(st_out[0] - top)
        total = jnp.sum(st_out[1] * weight, axis=0, keepdims=True)
        weighted = jnp.sum(st_out[2] * weight, axis=0, keepdims=True)
        norm = top + jnp.log(total) * LOG2_E
        delta = weighted / total
        finals[0][0:1, :] = norm
        finals[0][1:2, :] = delta
        rows = []
        for value in (norm, delta):
            for _ in range(3):
                part = value.astype(jnp.bfloat16).astype(jnp.float32)
                value = value - part
                rows += [part[:, j * HD : (j + 1) * HD] for j in range(TOK // HD)]
        rows.append(jnp.zeros((STAT_ROWS - len(rows), HD), jnp.float32))
        finals[1][...] = jnp.concatenate(rows, axis=0).astype(jnp.bfloat16)


def unpacked(rows):
    rows = rows.astype(jnp.float32)
    values = []
    for stat in range(2):
        lanes = []
        for j in range(TOK // HD):
            at = [9 * stat + 3 * part + j for part in range(3)]
            hi, mid, low = [rows[r : r + 1, :] for r in at]
            lanes.append(hi + (mid + low))
        values.append(jnp.concatenate(lanes, axis=1))
    return values


def query_kernel(scale, live, stat_ref, q_ref, g_ref, own_ref, mate_ref, far_ref, out_ref, acc, low, order):
    acc[...] = jnp.zeros_like(acc)
    norm = stat_ref[0:1, :]
    delta = stat_ref[1:2, :]
    for group, kv_ref in enumerate((own_ref, mate_ref, far_ref)):

        def visit(slots, kv_ref=kv_ref):
            for i, slot in enumerate(slots):
                logit = dot(kv_ref[slot, 0], q_ref[...], NT) * (scale * LOG2_E)
                prob = jnp.exp2(logit - norm)
                grad_prob = dot(kv_ref[slot, 1], g_ref[...], NT)
                low[i] = (prob * (grad_prob - delta)).astype(jnp.bfloat16)
            acc[...] += sum(
                dot(kv_ref[slot, 0], low[i], TN) for i, slot in enumerate(slots)
            )

        each_live(live, group * SLOTS, order, visit, WIDTHS)
    out_ref[...] = (acc[...].T * scale).astype(jnp.bfloat16)


def key_kernel(scale, last, live, k_ref, v_ref, *refs):
    refs, (prob_low, grad_low, order) = refs[:-3], refs[-3:]
    if last:
        qg_ref, stat_ref, acc_in, dk_out, dv_out, acc = refs
    else:
        qg_ref, acc_in, acc = refs
    acc[...] = acc_in[...]

    def visit(slots):
        queries, grads = [], []
        for i, slot in enumerate(slots):
            if last:
                query, grad = qg_ref[slot, 0], qg_ref[slot, 1]
                norm, delta = unpacked(stat_ref[slot])
            else:
                query = qg_ref[slot, pl.ds(0, TOK)]
                grad = qg_ref[slot, pl.ds(TOK, TOK)]
                norm, delta = unpacked(qg_ref[slot, pl.ds(2 * TOK, STAT_ROWS), :])
            logit = dot(k_ref[...], query, NT) * (scale * LOG2_E)
            prob = jnp.exp2(logit - norm)
            grad_prob = dot(v_ref[...], grad, NT)
            prob_low[i] = prob.astype(jnp.bfloat16)
            grad_low[i] = (prob * (grad_prob - delta)).astype(jnp.bfloat16)
            queries.append(query)
            grads.append(grad)
        acc[0] += sum(dot(grad_low[i], x, NN) for i, x in enumerate(queries))
        acc[1] += sum(dot(prob_low[i], x, NN) for i, x in enumerate(grads))

    each_live(live, 0, order, visit, WIDTHS)
    if last:
        dk_out[...] = (acc[0] * scale).astype(jnp.bfloat16)
        dv_out[...] = acc[1].astype(jnp.bfloat16)


def params():
    return pltpu.CompilerParams(vmem_limit_bytes=40 * 1024 * 1024)


def cost(pairs, matmuls):
    return pl.CostEstimate(
        flops=pairs * matmuls * 2 * TOK * TOK * HD,
        transcendentals=pairs * TOK * TOK,
        bytes_accessed=pairs * 4 * TOK * HD * 2,
    )


def run_stats(scale, live, q, g, kv, state, last):
    state_shape = jax.ShapeDtypeStruct((3, 8, TOK), jnp.float32)
    stat_shape = jax.ShapeDtypeStruct((2, TOK), jnp.float32)
    sent_shape = jax.ShapeDtypeStruct((STAT_ROWS, HD), jnp.bfloat16)

    def body(*refs):
        stats_kernel(scale, last, *refs)

    return pl.pallas_call(
        body,
        out_shape=(state_shape, stat_shape, sent_shape) if last else (state_shape,),
        in_specs=[SMEM, VMEM, VMEM, VMEM, VMEM],
        out_specs=(VMEM,) * 3 if last else (VMEM,),
        scratch_shapes=[pltpu.SMEM((SLOTS + 1,), jnp.int32)],
        compiler_params=params(),
        cost_estimate=cost(SLOTS, 2),
        name="row_stats",
    )(live, q, g, kv, state)


def run_query(scale, live, stat, q, g, groups):
    def body(*refs):
        query_kernel(scale, *refs)

    return pl.pallas_call(
        body,
        out_shape=jax.ShapeDtypeStruct((TOK, HD), jnp.bfloat16),
        in_specs=[SMEM] + [VMEM] * 6,
        out_specs=VMEM,
        scratch_shapes=[
            pltpu.VMEM((HD, TOK), jnp.float32),
            pltpu.VMEM((MOST, TOK, TOK), jnp.bfloat16),
            pltpu.SMEM((SLOTS + 1,), jnp.int32),
        ],
        compiler_params=params(),
        cost_estimate=cost(3 * SLOTS, 3),
        name="grad_dq",
    )(live, stat, q, g, *groups)


def run_key(scale, live, k, v, given, acc, last):
    acc_shape = jax.ShapeDtypeStruct((2, TOK, HD), jnp.float32)
    low_shape = jax.ShapeDtypeStruct((TOK, HD), jnp.bfloat16)

    def body(*refs):
        key_kernel(scale, last, *refs)

    return pl.pallas_call(
        body,
        out_shape=(low_shape, low_shape, acc_shape) if last else (acc_shape,),
        in_specs=[SMEM] + [VMEM] * (3 + len(given)),
        out_specs=(VMEM, VMEM, VMEM) if last else (VMEM,),
        scratch_shapes=[
            pltpu.VMEM((MOST, TOK, TOK), jnp.bfloat16),
            pltpu.VMEM((MOST, TOK, TOK), jnp.bfloat16),
            pltpu.SMEM((SLOTS + 1,), jnp.int32),
        ],
        compiler_params=params(),
        cost_estimate=cost(SLOTS, 4),
        name="grad_key",
    )(live, k, v, *given, acc)


def live_slots(key_tiles, tile_count, my_lat, my_z, my_y):
    columns, real = slot_columns(my_z, my_y)
    far_lat = jnp.where(my_lat % 2 == 1, my_lat + 1, my_lat - 1)
    bands = jnp.stack([my_lat, my_lat ^ 1, far_lat])
    band_real = (bands >= 0) & (bands < LAT)
    ids = (bands[:, None] * LON + columns[None, :]).reshape(-1)
    slot_real = (band_real[:, None] & real[None, :]).reshape(-1)
    table = key_tiles.reshape(LAT * LON, -1)
    totals = tile_count.reshape(-1)
    places = jnp.arange(table.shape[1], dtype=jnp.int32)
    own_id = my_lat * LON + my_z * Y + my_y
    own_list = lax.dynamic_index_in_dim(table, own_id, 0, keepdims=False)
    own_total = lax.dynamic_index_in_dim(totals, own_id, 0, keepdims=False)
    i_list = jnp.any(
        (own_list[None, :] == ids[:, None]) & (places < own_total)[None, :], axis=1
    )
    safe = jnp.clip(ids, 0, LAT * LON - 1)
    lists_me = jnp.any(
        (table[safe] == own_id) & (places[None, :] < totals[safe][:, None]), axis=1
    )
    live_keys = (i_list & slot_real).astype(jnp.int32)
    live_queries = (lists_me & slot_real).astype(jnp.int32)
    return live_keys.reshape(3, SLOTS), live_queries.reshape(3, SLOTS)


def per_device(queries, keys, values, cotangent, key_tiles, tile_count):
    scale = HD ** (-0.5)
    my_lat = lax.axis_index("lat")
    my_lon = lax.axis_index("lon")
    my_z, my_y = my_lon // Y, my_lon % Y
    q = queries.reshape(TOK, HD)
    k = keys.reshape(TOK, HD)
    v = values.reshape(TOK, HD)
    g = cotangent.reshape(TOK, HD)

    place = lax.optimization_barrier((my_lat, my_z, my_y))
    live_k, live_q = live_slots(key_tiles, tile_count, *place)

    kv = lax.optimization_barrier(jnp.stack([k, v]))
    qg = jnp.stack([q, g])
    qg = lax.optimization_barrier(qg)
    far_kv = permuted(kv, cross_rule)
    own_kv = spread_own(kv, my_y)
    far_kvs = spread_far(kv, far_kv, my_z, my_y)
    mate_kv = permuted(own_kv, swap_rule)
    far_qg = permuted(qg, cross_rule)
    far_qgs = spread_far(qg, far_qg, my_z, my_y)

    tall = qg.reshape(2 * TOK, HD)
    tall_before = permuted(tall, z_rule(1))
    tall_after = permuted(tall, z_rule(-1))
    payload = run_pack(my_y, tall, tall_before, tall_after, PACK)

    blank = jnp.zeros((8, TOK), jnp.float32)
    state = jnp.stack([blank + NEG_BIG, blank, blank])
    (state,) = run_stats(scale, live_k[0], q, g, own_kv, state, False)
    (state,) = run_stats(scale, live_k[1], q, g, mate_kv, state, False)
    _, stat, sent = run_stats(scale, live_k[2], q, g, far_kvs, state, True)

    sent_before = permuted(sent, z_rule(1))
    sent_after = permuted(sent, z_rule(-1))
    payload = run_put(my_y, sent, sent_before, sent_after, payload)
    own_qg = exchanged(payload)
    mate_qg = permuted(own_qg, swap_rule)
    far_stats = permuted(own_qg[:, 2 * TOK :], cross_rule)
    grad_query = run_query(
        scale, live_k.reshape(-1), stat, q, g, (own_kv, mate_kv, far_kvs)
    )

    acc = jnp.zeros((2, TOK, HD), jnp.float32)
    (acc,) = run_key(scale, live_q[0], k, v, (own_qg,), acc, False)
    (acc,) = run_key(scale, live_q[1], k, v, (mate_qg,), acc, False)
    grad_key, grad_value, _ = run_key(
        scale, live_q[2], k, v, (far_qgs, far_stats), acc, True
    )
    out_shape = (1, 1, TOK, HD)
    return (
        grad_query.reshape(out_shape),
        grad_key.reshape(out_shape),
        grad_value.reshape(out_shape),
    )


def solution(mesh):
    tile = P("lat", "lon", None, None)

    return jax.shard_map(
        per_device,
        mesh=mesh,
        in_specs=(tile, tile, tile, tile, P(), P()),
        out_specs=(tile, tile, tile),
        check_vma=False,
    )
```

```python
import jax
import jax.numpy as jnp
from jax import lax
from jax.experimental import pallas as pl
from jax.experimental.pallas import tpu as pltpu
from jax.sharding import PartitionSpec as P


Y = 4
ZL = 8
LON = 32
LAT = 16
TOK = 384
HD = 128
SLOTS = 8
NEG_BIG = -1e30
AXES = ("lon", "lat")
WIDTHS = (7, 3, 1)
STAT_WIDTHS = (2, 1)
MOST = max(WIDTHS)
LOG2_E = 1.4426950408889634
STAT_ROWS = 32
PACK = 2 * TOK + STAT_ROWS


SMEM = pl.BlockSpec(memory_space=pltpu.SMEM)
VMEM = pl.BlockSpec(memory_space=pltpu.VMEM)


def cross_of(lat):
    other = lat + 1 if lat % 2 else lat - 1
    return other if 0 <= other < LAT else None


def pairs_of(rule):
    pairs = []
    for lon in range(LON):
        for lat in range(LAT):
            to = rule(lon // Y, lon % Y, lat)
            if to is not None:
                z, y, band = to
                pairs.append((lon * LAT + lat, (z * Y + y) * LAT + band))
    return pairs


def swap_rule(z, y, lat):
    return (z, y, lat ^ 1)


def cross_rule(z, y, lat):
    other = cross_of(lat)
    return None if other is None else (z, y, other)


def z_rule(step):
    unused = 0 if step > 0 else Y - 1

    def rule(z, y, lat):
        return None if y == unused else ((z + step) % ZL, y, lat)

    return rule


def far_z_rule(step):
    unused = 0 if step > 0 else Y - 1

    def rule(z, y, lat):
        if y == unused:
            return None
        if 0 <= z + step < ZL:
            return (z + step, y, lat)
        other = cross_of(lat)
        return None if other is None else ((z + step) % ZL, y, other)

    return rule


def permuted(x, rule):
    return lax.ppermute(x, AXES, pairs_of(rule))


def pack_kernel(my_y, here, before, after, out):
    for peer in range(Y):
        out[peer, 0] = here[...]

        @pl.when(peer < my_y[0])
        def _():
            out[peer, 1] = before[...]

        @pl.when(peer >= my_y[0])
        def _():
            out[peer, 1] = after[...]


def run_pack(my_y, here, before, after):
    return pl.pallas_call(
        pack_kernel,
        out_shape=jax.ShapeDtypeStruct((Y, 2) + here.shape, here.dtype),
        in_specs=[SMEM] + [VMEM] * 3,
        out_specs=VMEM,
        name="pack",
    )(my_y.reshape(1), here, before, after)


def pack_ahead_kernel(my_y, here, before, after, *outs):
    for ahead, out in enumerate(outs, 1):
        out[0] = here[...]

        @pl.when(my_y[0] + ahead >= Y)
        def _():
            out[1] = before[...]

        @pl.when(my_y[0] + ahead < Y)
        def _():
            out[1] = after[...]


def collect_kernel(my_y, here, *refs):
    arrived, out = refs[:-1], refs[-1]
    out[my_y[0], 0] = here[...]
    out[my_y[0], 1] = here[...]
    for ahead, pair in enumerate(arrived, 1):
        out[(my_y[0] + Y - ahead) % Y] = pair[...]


def y_rule(ahead):
    def rule(z, y, lat):
        return (z, (y + ahead) % Y, lat)

    return rule


def spread_y_by_permutes(here, before, after, my_y):
    mine = my_y.reshape(1)
    pair = jax.ShapeDtypeStruct((2,) + here.shape, here.dtype)
    outgoing = pl.pallas_call(
        pack_ahead_kernel,
        out_shape=(pair,) * (Y - 1),
        in_specs=[SMEM] + [VMEM] * 3,
        out_specs=(VMEM,) * (Y - 1),
        name="ahead",
    )(mine, here, before, after)
    arrived = [permuted(x, y_rule(ahead)) for ahead, x in enumerate(outgoing, 1)]
    got = pl.pallas_call(
        collect_kernel,
        out_shape=jax.ShapeDtypeStruct((Y, 2) + here.shape, here.dtype),
        in_specs=[SMEM] + [VMEM] * Y,
        out_specs=VMEM,
        name="collect",
    )(mine, here, *arrived)
    return got.reshape((SLOTS,) + here.shape)


def spread_y(here, before, after, my_y):
    groups = [[z * Y + y for y in range(Y)] for z in range(ZL)]
    payload = run_pack(my_y, here, before, after)
    got = lax.all_to_all(
        payload, "lon", 0, 0, axis_index_groups=groups, tiled=True
    )
    return got.reshape((SLOTS,) + here.shape)


def spread_own(here, my_y):
    before = permuted(here, z_rule(1))
    after = permuted(here, z_rule(-1))
    return spread_y(here, before, after, my_y)


def spread_far(here, far, my_z, my_y):
    before = permuted(jnp.where(my_z == ZL - 1, here, far), far_z_rule(1))
    after = permuted(jnp.where(my_z == 0, here, far), far_z_rule(-1))
    return spread_y(far, before, after, my_y)


def slot_columns(my_z, my_y):
    sender = jnp.arange(Y, dtype=jnp.int32)
    near = my_z * Y + sender
    beside = (my_z + jnp.where(sender > my_y, -1, 1)) % ZL * Y + sender
    columns = jnp.stack([near, beside], axis=1).reshape(SLOTS)
    real = jnp.stack([sender >= 0, sender != my_y], axis=1).reshape(SLOTS)
    return columns, real


NT = (((1,), (1,)), ((), ()))
NN = (((1,), (0,)), ((), ()))
TN = (((0,), (0,)), ((), ()))


def dot(a, b, dims):
    return lax.dot_general(a, b, dims, preferred_element_type=jnp.float32)


def each_live(live, base, order, visit, widths):
    order[SLOTS] = 0
    for slot in range(SLOTS):

        @pl.when(live[base + slot] != 0)
        def _(slot=slot):
            count = order[SLOTS]
            order[count] = slot
            order[SLOTS] = count + 1

    count = order[SLOTS]
    start = 0
    for width in widths:
        rounds = (count - start) // width

        def several(i, carry, width=width, start=start):
            visit([order[start + i * width + j] for j in range(width)])
            return carry

        lax.fori_loop(0, rounds, several, 0)
        start = start + rounds * width


def stats_kernel(scale, last, live, q_ref, g_ref, kv_ref, st_in, st_out, *rest):
    finals, order = rest[:-1], rest[-1]
    st_out[...] = st_in[...]

    def visit(slots):
        logits, grad_probs = [], []
        for slot in slots:
            logits.append(dot(kv_ref[slot, 0], q_ref[...], NT) * (scale * LOG2_E))
            grad_probs.append(dot(kv_ref[slot, 1], g_ref[...], NT))
        logits = [x.reshape(TOK // 8, 8, TOK) for x in logits]
        grad_probs = [x.reshape(TOK // 8, 8, TOK) for x in grad_probs]
        old_max = new_max = st_out[0]
        for logit in logits:
            new_max = jnp.maximum(new_max, jnp.max(logit, axis=0))
        rescale = jnp.exp2(old_max - new_max)
        total = st_out[1] * rescale
        weighted = st_out[2] * rescale
        for logit, grad_prob in zip(logits, grad_probs):
            power = jnp.exp2(logit - new_max[None])
            total += jnp.sum(power, axis=0)
            weighted += jnp.sum(power * grad_prob, axis=0)
        st_out[0] = new_max
        st_out[1] = total
        st_out[2] = weighted

    each_live(live, 0, order, visit, STAT_WIDTHS)
    if last:
        top = jnp.max(st_out[0], axis=0, keepdims=True)
        weight = jnp.exp2(st_out[0] - top)
        total = jnp.sum(st_out[1] * weight, axis=0, keepdims=True)
        weighted = jnp.sum(st_out[2] * weight, axis=0, keepdims=True)
        norm = top + jnp.log(total) * LOG2_E
        delta = weighted / total
        finals[0][0:1, :] = norm
        finals[0][1:2, :] = delta
        rows = []
        for value in (norm, delta):
            for _ in range(3):
                part = value.astype(jnp.bfloat16).astype(jnp.float32)
                value = value - part
                rows += [part[:, j * HD : (j + 1) * HD] for j in range(TOK // HD)]
        rows.append(jnp.zeros((STAT_ROWS - len(rows), HD), jnp.float32))
        pack = finals[1]
        pack[0:TOK, :] = q_ref[...]
        pack[TOK : 2 * TOK, :] = g_ref[...]
        pack[2 * TOK :, :] = jnp.concatenate(rows, axis=0).astype(jnp.bfloat16)


def unpacked(rows):
    rows = rows.astype(jnp.float32)
    values = []
    for stat in range(2):
        lanes = []
        for j in range(TOK // HD):
            at = [9 * stat + 3 * part + j for part in range(3)]
            hi, mid, low = [rows[r : r + 1, :] for r in at]
            lanes.append(hi + (mid + low))
        values.append(jnp.concatenate(lanes, axis=1))
    return values


def query_kernel(scale, live, stat_ref, q_ref, g_ref, own_ref, mate_ref, far_ref, out_ref, acc, low, order):
    acc[...] = jnp.zeros_like(acc)
    norm = stat_ref[0:1, :]
    delta = stat_ref[1:2, :]
    for group, kv_ref in enumerate((own_ref, mate_ref, far_ref)):

        def visit(slots, kv_ref=kv_ref):
            for i, slot in enumerate(slots):
                logit = dot(kv_ref[slot, 0], q_ref[...], NT) * (scale * LOG2_E)
                prob = jnp.exp2(logit - norm)
                grad_prob = dot(kv_ref[slot, 1], g_ref[...], NT)
                low[i] = (prob * (grad_prob - delta)).astype(jnp.bfloat16)
            acc[...] += sum(
                dot(kv_ref[slot, 0], low[i], TN) for i, slot in enumerate(slots)
            )

        each_live(live, group * SLOTS, order, visit, WIDTHS)
    out_ref[...] = (acc[...].T * scale).astype(jnp.bfloat16)


def key_kernel(scale, last, live, k_ref, v_ref, *refs):
    refs, (prob_low, grad_low, order) = refs[:-3], refs[-3:]
    if last:
        qg_ref, stat_ref, acc_in, dk_out, dv_out, acc = refs
    else:
        qg_ref, acc_in, acc = refs
    acc[...] = acc_in[...]

    def visit(slots):
        queries, grads = [], []
        for i, slot in enumerate(slots):
            if last:
                query, grad = qg_ref[slot, 0], qg_ref[slot, 1]
                norm, delta = unpacked(stat_ref[slot])
            else:
                query = qg_ref[slot, pl.ds(0, TOK)]
                grad = qg_ref[slot, pl.ds(TOK, TOK)]
                norm, delta = unpacked(qg_ref[slot, pl.ds(2 * TOK, STAT_ROWS), :])
            logit = dot(k_ref[...], query, NT) * (scale * LOG2_E)
            prob = jnp.exp2(logit - norm)
            grad_prob = dot(v_ref[...], grad, NT)
            prob_low[i] = prob.astype(jnp.bfloat16)
            grad_low[i] = (prob * (grad_prob - delta)).astype(jnp.bfloat16)
            queries.append(query)
            grads.append(grad)
        acc[0] += sum(dot(grad_low[i], x, NN) for i, x in enumerate(queries))
        acc[1] += sum(dot(prob_low[i], x, NN) for i, x in enumerate(grads))

    each_live(live, 0, order, visit, WIDTHS)
    if last:
        dk_out[...] = (acc[0] * scale).astype(jnp.bfloat16)
        dv_out[...] = acc[1].astype(jnp.bfloat16)


def params(mib):
    return pltpu.CompilerParams(vmem_limit_bytes=mib * 1024 * 1024)


def cost(pairs, matmuls):
    return pl.CostEstimate(
        flops=pairs * matmuls * 2 * TOK * TOK * HD,
        transcendentals=pairs * TOK * TOK,
        bytes_accessed=pairs * 4 * TOK * HD * 2,
    )


def run_stats(scale, live, q, g, kv, state, last):
    state_shape = jax.ShapeDtypeStruct((3, 8, TOK), jnp.float32)
    stat_shape = jax.ShapeDtypeStruct((2, TOK), jnp.float32)
    pack_shape = jax.ShapeDtypeStruct((PACK, HD), jnp.bfloat16)

    def body(*refs):
        stats_kernel(scale, last, *refs)

    return pl.pallas_call(
        body,
        out_shape=(state_shape, stat_shape, pack_shape) if last else (state_shape,),
        in_specs=[SMEM, VMEM, VMEM, VMEM, VMEM],
        out_specs=(VMEM,) * 3 if last else (VMEM,),
        scratch_shapes=[pltpu.SMEM((SLOTS + 1,), jnp.int32)],
        compiler_params=params(12),
        cost_estimate=cost(SLOTS, 2),
        name="row_stats",
    )(live, q, g, kv, state)


def run_query(scale, live, stat, q, g, groups):
    def body(*refs):
        query_kernel(scale, *refs)

    return pl.pallas_call(
        body,
        out_shape=jax.ShapeDtypeStruct((TOK, HD), jnp.bfloat16),
        in_specs=[SMEM] + [VMEM] * 6,
        out_specs=VMEM,
        scratch_shapes=[
            pltpu.VMEM((HD, TOK), jnp.float32),
            pltpu.VMEM((MOST, TOK, TOK), jnp.bfloat16),
            pltpu.SMEM((SLOTS + 1,), jnp.int32),
        ],
        compiler_params=params(30),
        cost_estimate=cost(3 * SLOTS, 3),
        name="grad_dq",
    )(live, stat, q, g, *groups)


def run_key(scale, live, k, v, given, acc, last):
    acc_shape = jax.ShapeDtypeStruct((2, TOK, HD), jnp.float32)
    low_shape = jax.ShapeDtypeStruct((TOK, HD), jnp.bfloat16)

    def body(*refs):
        key_kernel(scale, last, *refs)

    return pl.pallas_call(
        body,
        out_shape=(low_shape, low_shape, acc_shape) if last else (acc_shape,),
        in_specs=[SMEM] + [VMEM] * (3 + len(given)),
        out_specs=(VMEM, VMEM, VMEM) if last else (VMEM,),
        scratch_shapes=[
            pltpu.VMEM((MOST, TOK, TOK), jnp.bfloat16),
            pltpu.VMEM((MOST, TOK, TOK), jnp.bfloat16),
            pltpu.SMEM((SLOTS + 1,), jnp.int32),
        ],
        compiler_params=params(30),
        cost_estimate=cost(SLOTS, 4),
        name="grad_key",
    )(live, k, v, *given, acc)


def live_slots(key_tiles, tile_count, my_lat, my_z, my_y):
    columns, real = slot_columns(my_z, my_y)
    far_lat = jnp.where(my_lat % 2 == 1, my_lat + 1, my_lat - 1)
    bands = jnp.stack([my_lat, my_lat ^ 1, far_lat])
    band_real = (bands >= 0) & (bands < LAT)
    ids = (bands[:, None] * LON + columns[None, :]).reshape(-1)
    slot_real = (band_real[:, None] & real[None, :]).reshape(-1)
    table = key_tiles.reshape(LAT * LON, -1)
    totals = tile_count.reshape(-1)
    places = jnp.arange(table.shape[1], dtype=jnp.int32)
    own_id = my_lat * LON + my_z * Y + my_y
    own_list = lax.dynamic_index_in_dim(table, own_id, 0, keepdims=False)
    own_total = lax.dynamic_index_in_dim(totals, own_id, 0, keepdims=False)
    i_list = jnp.any(
        (own_list[None, :] == ids[:, None]) & (places < own_total)[None, :], axis=1
    )
    safe = jnp.clip(ids, 0, LAT * LON - 1)
    lists_me = jnp.any(
        (table[safe] == own_id) & (places[None, :] < totals[safe][:, None]), axis=1
    )
    live_keys = (i_list & slot_real).astype(jnp.int32)
    live_queries = (lists_me & slot_real).astype(jnp.int32)
    return live_keys.reshape(3, SLOTS), live_queries.reshape(3, SLOTS)


def per_device(queries, keys, values, cotangent, key_tiles, tile_count):
    scale = HD ** (-0.5)
    my_lat = lax.axis_index("lat")
    my_lon = lax.axis_index("lon")
    my_z, my_y = my_lon // Y, my_lon % Y
    q = queries.reshape(TOK, HD)
    k = keys.reshape(TOK, HD)
    v = values.reshape(TOK, HD)
    g = cotangent.reshape(TOK, HD)

    place = lax.optimization_barrier((my_lat, my_z, my_y))
    live_k, live_q = live_slots(key_tiles, tile_count, *place)

    kv = lax.optimization_barrier(jnp.stack([k, v]))
    qg = jnp.stack([q, g])
    qg = lax.optimization_barrier(qg)
    far_kv = permuted(kv, cross_rule)
    own_kv = spread_own(kv, my_y)
    far_kvs = spread_far(kv, far_kv, my_z, my_y)
    mate_kv = permuted(own_kv, swap_rule)
    far_qg = permuted(qg, cross_rule)
    far_qgs = spread_far(qg, far_qg, my_z, my_y)

    blank = jnp.zeros((8, TOK), jnp.float32)
    state = jnp.stack([blank + NEG_BIG, blank, blank])
    (state,) = run_stats(scale, live_k[0], q, g, own_kv, state, False)
    (state,) = run_stats(scale, live_k[1], q, g, mate_kv, state, False)
    _, stat, pack = run_stats(scale, live_k[2], q, g, far_kvs, state, True)

    pack_before = permuted(pack, z_rule(1))
    pack_after = permuted(pack, z_rule(-1))
    own_qg = spread_y_by_permutes(pack, pack_before, pack_after, my_y)
    mate_qg = permuted(own_qg, swap_rule)
    far_stats = permuted(own_qg[:, 2 * TOK :], cross_rule)
    grad_query = run_query(
        scale, live_k.reshape(-1), stat, q, g, (own_kv, mate_kv, far_kvs)
    )

    acc = jnp.zeros((2, TOK, HD), jnp.float32)
    (acc,) = run_key(scale, live_q[0], k, v, (own_qg,), acc, False)
    (acc,) = run_key(scale, live_q[1], k, v, (mate_qg,), acc, False)
    grad_key, grad_value, _ = run_key(
        scale, live_q[2], k, v, (far_qgs, far_stats), acc, True
    )
    out_shape = (1, 1, TOK, HD)
    return (
        grad_query.reshape(out_shape),
        grad_key.reshape(out_shape),
        grad_value.reshape(out_shape),
    )


def solution(mesh):
    tile = P("lat", "lon", None, None)

    return jax.shard_map(
        per_device,
        mesh=mesh,
        in_specs=(tile, tile, tile, tile, P(), P()),
        out_specs=(tile, tile, tile),
        check_vma=False,
    )
```
